128 devices in a mesh: ctx: 32 (over y, x, core), head: 4 (over z).
Axes of the slice: x: 4, y: 4, z: 4, core: 2. Of those that a mesh axis runs over, the one named last changes fastest.
Arguments:
- attn_query: bfloat16 [16384, 32, 128], P('ctx', 'head'), may hold values from -6 to 6
- attn_key: bfloat16 [16384, 8, 128], P('ctx', 'head'), may hold values from -6 to 6
- attention_value: bfloat16 [16384, 8, 128], P('ctx', 'head'), may hold values from -6 to 6
- delta_query: bfloat16 [16384, 32, 128], P('ctx', 'head'), may hold values from -6 to 6
- delta_key: bfloat16 [16384, 32, 128], P('ctx', 'head'), may hold values from -6 to 6
- delta_value: bfloat16 [16384, 32, 128], P('ctx', 'head'), may hold values from -6 to 6
- log_decay: float32 [32, 16384], P('head', 'ctx'), may hold values from -0.8 to 0, as said below
- beta_gate: float32 [32, 16384], P('head', 'ctx'), may hold values from 0.1 to 0.9
Outputs:
- attn_out: bfloat16 [16384, 4096], P(('ctx', 'head'))
- delta_out: bfloat16 [16384, 4096], P(('ctx', 'head'))
The draws below stay inside these ranges and needn't reach their ends.
Inputs may be any that keep to these rules, and one draw needn't show every extreme that they name: `log_decay`: each entry is the natural logarithm of a decay factor of one head at one token.
All inputs are finite; a program needn't handle non-finite values.
Results may differ from the reference program's by a relative error of at most 0.0045.
Values may be sent and summed in bfloat16 or wider, within the bound.
No kernel may reach another device: no remote copies, remote signals or barrier semaphores. Data moves between devices by JAX's collectives and lax.ppermute only.
A program may use at most 128 MiB of HBM per device.

```python
import math
import jax
import jax.numpy as jnp
from jax import lax

HEAD_SIZE = 128
QUERY_HEADS = 32
KEY_VALUE_HEADS = 8
DELTA_HEADS = 32
WINDOW = 1024
SPAN = 64
TOK_DEV = 512
SEQUENCE_TOKENS = 16384


def draw_attn_query(key, part):
    random_key = jax.random.fold_in(key, 1)
    sampled_values = jax.random.truncated_normal(random_key, -6.0, 6.0, (SEQUENCE_TOKENS, QUERY_HEADS, HEAD_SIZE), jnp.float32)
    return sampled_values.astype(jnp.bfloat16)


def draw_attn_key(key, part):
    random_key = jax.random.fold_in(key, 2)
    sampled_values = jax.random.truncated_normal(random_key, -6.0, 6.0, (SEQUENCE_TOKENS, KEY_VALUE_HEADS, HEAD_SIZE), jnp.float32)
    return sampled_values.astype(jnp.bfloat16)


def draw_delta_key(key, part):
    sub_rank = max(2, HEAD_SIZE // 8)
    head_keys = jax.random.split(jax.random.fold_in(key, 31), DELTA_HEADS)
    orders = jax.vmap(lambda one_key: jax.random.permutation(one_key, HEAD_SIZE))(head_keys)
    inside = orders < sub_rank
    spread_level = math.sqrt(sub_rank / SEQUENCE_TOKENS)
    scale_table = jnp.where(inside, 1.0, spread_level).astype(jnp.float32)
    random_key = jax.random.fold_in(key, 32)
    sampled_values = jax.random.truncated_normal(random_key, -6.0, 6.0, (SEQUENCE_TOKENS, DELTA_HEADS, HEAD_SIZE), jnp.float32)
    sampled_values = sampled_values * scale_table[None, :, :]
    return sampled_values.astype(jnp.bfloat16)


def draw_log_decay(key, part):
    fast_count = DELTA_HEADS // 2
    rank_order = jax.random.permutation(jax.random.fold_in(key, 21), DELTA_HEADS)
    quick_head = rank_order < fast_count
    fast_rate = jnp.exp(jax.random.uniform(jax.random.fold_in(key, 22), (DELTA_HEADS,), jnp.float32, math.log(1.0 / 50.0), math.log(1.0 / 30.0)))
    slow_rate = jnp.exp(jax.random.uniform(jax.random.fold_in(key, 23), (DELTA_HEADS,), jnp.float32, math.log(0.05), math.log(0.5))) / SEQUENCE_TOKENS
    decay_speed = jnp.where(quick_head, fast_rate, slow_rate)
    multiplier = jnp.exp(jax.random.uniform(jax.random.fold_in(key, 24), (DELTA_HEADS, SEQUENCE_TOKENS // TOK_DEV), jnp.float32, math.log(0.6), math.log(1.7)))
    multiplier = jnp.repeat(multiplier, TOK_DEV, axis=1)
    third_length = SEQUENCE_TOKENS // 3
    spike_position = jnp.arange(3)[None, :] * third_length + jax.random.randint(jax.random.fold_in(key, 25), (DELTA_HEADS, 3), 0, third_length)
    spike_drop = jnp.log(jax.random.uniform(jax.random.fold_in(key, 26), (DELTA_HEADS, 3), jnp.float32, 0.5, 0.8))
    token_position = jnp.arange(SEQUENCE_TOKENS)
    spike_sum = jnp.sum(jnp.where(token_position[None, None, :] == spike_position[:, :, None], spike_drop[:, :, None], 0.0), axis=1)
    sampled_values = jnp.where(quick_head[:, None], 0.0, spike_sum) - decay_speed[:, None] * multiplier
    return sampled_values.astype(jnp.float32)


def block_levels(own_key, extent, cuts, smallest, largest):
    def one(position, blocks):
        heights = jax.random.uniform(jax.random.fold_in(jax.random.fold_in(own_key, 6), position), (blocks,), jnp.float32, smallest / len(cuts), largest / len(cuts))
        return jnp.repeat(jnp.exp(heights), extent[position] // blocks).reshape((-1,) + (1,) * (len(extent) - position - 1))

    level = one(*cuts[0])
    for cut in cuts[1:]:
        level = level * one(*cut)
    return level


def noise(rng, extent, deviation, reach, pieces=(), held_as=jnp.bfloat16):
    level = block_levels(rng, extent, pieces, -0.22, 0.18) if pieces else 1.0
    array = jax.random.normal(rng, extent, jnp.float32) * deviation * level
    return jnp.minimum(jnp.maximum(array, -reach), reach).astype(held_as)


def setup_inputs(seed: int = 0) -> dict:
    key_list = jax.random.split(jax.random.key(seed), 9)
    return {
        "attn_query": draw_attn_query(jax.random.fold_in(key_list[8], 71), 0),
        "attn_key": draw_attn_key(jax.random.fold_in(key_list[8], 71), 0),
        "attention_value": noise(key_list[2], (SEQUENCE_TOKENS, KEY_VALUE_HEADS, HEAD_SIZE), 1.0, 6.0, ((0, 32), (1, 4))),
        "delta_query": noise(key_list[3], (SEQUENCE_TOKENS, DELTA_HEADS, HEAD_SIZE), 1.0, 6.0, ((0, 32), (1, 4))),
        "delta_key": draw_delta_key(jax.random.fold_in(key_list[8], 71), 0),
        "delta_value": noise(key_list[5], (SEQUENCE_TOKENS, DELTA_HEADS, HEAD_SIZE), 1.0, 6.0, ((0, 32), (1, 4))),
        "log_decay": draw_log_decay(jax.random.fold_in(key_list[8], 71), 0),
        "beta_gate": jnp.clip(0.1 + 0.79999997 * jax.random.uniform(key_list[7], (DELTA_HEADS, SEQUENCE_TOKENS), jnp.float32) ** block_levels(key_list[7], (DELTA_HEADS, SEQUENCE_TOKENS), ((0, 4), (1, 32)), -0.2, 0.2), 0.1, 0.9),
    }


norm_epsilon = 1e-06

def product(form, left, right):
    return jnp.einsum(form, left, right, precision=lax.Precision.HIGHEST)

def normalize(tensor, scale_factor):
    widened = tensor.astype(jnp.float32)
    return widened / jnp.sqrt(lax.optimization_barrier(jnp.sum(widened * widened, axis=-1, keepdims=True)) + norm_epsilon) * scale_factor

def invert_unit(strict):
    span_len = strict.shape[-1]
    identity = jnp.eye(span_len, dtype=strict.dtype)
    inverse = identity - strict
    power_term = strict
    for level in range(1, max(1, (span_len - 1).bit_length())):
        power_term = product('hij,hjk->hik', power_term, power_term)
        inverse = inverse + product('hij,hjk->hik', inverse, power_term)
    return inverse

def prepare(query_unit, key_unit, beta_rows, log_rows):
    span_len = log_rows.shape[1]
    cumulative = jnp.cumsum(log_rows, axis=1)
    row_index = jnp.arange(span_len, dtype=jnp.int32)[:, None]
    col_index = jnp.arange(span_len, dtype=jnp.int32)[None, :]
    log_gap = cumulative[:, :, None] - cumulative[:, None, :]
    decay_ratio = jnp.exp(jnp.where(row_index >= col_index, log_gap, -jnp.inf))
    key_inner = product('hcd,hed->hce', key_unit, key_unit)
    strict = jnp.where(row_index > col_index, beta_rows[:, :, None] * decay_ratio * key_inner, 0.0)
    causal = product('hcd,hed->hce', query_unit, key_unit) * decay_ratio
    return (cumulative, invert_unit(strict), causal)

def advance(carried, query_unit, key_unit, value_rows, beta_rows, prepared):
    cumulative, inverse, causal = prepared
    leading = jnp.exp(cumulative)
    projected = product('hcd,hvd->hcv', key_unit, carried)
    right_side = beta_rows[:, :, None] * (value_rows - leading[:, :, None] * projected)
    weighted = product('hce,hev->hcv', inverse, right_side)
    result = leading[:, :, None] * product('hcd,hvd->hcv', query_unit, carried) + product('hts,hsv->htv', causal, weighted)
    trailing = jnp.exp(cumulative[:, -1:] - cumulative)
    updated = jnp.exp(cumulative[:, -1])[:, None, None] * carried + product('hsv,hsd->hvd', trailing[:, :, None] * weighted, key_unit)
    return (updated, result)

def to_spans(tensor, span_len):
    return tensor.reshape(tensor.shape[0] // span_len, span_len, tensor.shape[1], tensor.shape[2]).transpose(0, 2, 1, 3)

def gate_spans(tensor, span_len):
    return tensor.reshape(tensor.shape[0], tensor.shape[1] // span_len, span_len).transpose(1, 0, 2)

def from_spans(tensor):
    return tensor.transpose(0, 2, 1, 3).reshape(tensor.shape[0] * tensor.shape[2], tensor.shape[1] * tensor.shape[3])

def reference(attn_query, attn_key, attention_value, delta_query, delta_key, delta_value, log_decay, beta_gate):
    block_length = math.gcd(512, SEQUENCE_TOKENS)
    group_count = QUERY_HEADS // KEY_VALUE_HEADS
    key_padded = jnp.pad(attn_key, ((WINDOW, 0), (0, 0), (0, 0)))
    value_padded = jnp.pad(attention_value, ((WINDOW, 0), (0, 0), (0, 0)))

    def attend_block(block_index):
        block_start = block_index * block_length
        query_tile_block = lax.dynamic_slice_in_dim(attn_query, block_start, block_length, 0)
        query_tile_block = query_tile_block.reshape(block_length, KEY_VALUE_HEADS, group_count, HEAD_SIZE).astype(jnp.float32)
        key_block = lax.dynamic_slice_in_dim(key_padded, block_start, WINDOW + block_length, 0).astype(jnp.float32)
        value_block = lax.dynamic_slice_in_dim(value_padded, block_start, WINDOW + block_length, 0).astype(jnp.float32)
        scores = jnp.einsum('qgrd,kgd->grqk', query_tile_block, key_block) * (1.0 / math.sqrt(HEAD_SIZE))
        query_pos = block_start + jnp.arange(block_length, dtype=jnp.int32)
        key_pos = block_start - WINDOW + jnp.arange(WINDOW + block_length, dtype=jnp.int32)
        allowed = (key_pos[None, :] <= query_pos[:, None]) & (key_pos[None, :] > query_pos[:, None] - WINDOW) & (key_pos[None, :] >= 0)
        scores = jnp.where(allowed, scores, -jnp.inf)
        row_max = lax.optimization_barrier(jnp.max(scores, axis=-1, keepdims=True))
        unnormed = jnp.exp(scores - row_max)
        row_total = lax.optimization_barrier(jnp.sum(unnormed, axis=-1))
        weights = unnormed.astype(jnp.bfloat16)
        mixed_out = jnp.einsum('grqk,kgd->qgrd', weights.astype(jnp.float32), value_block)
        mixed_out = mixed_out / jnp.transpose(row_total, (2, 0, 1))[..., None]
        return mixed_out.reshape(block_length, QUERY_HEADS * HEAD_SIZE).astype(jnp.bfloat16)
    attn_blocks = lax.map(attend_block, jnp.arange(SEQUENCE_TOKENS // block_length, dtype=jnp.int32))
    attn_out = attn_blocks.reshape(SEQUENCE_TOKENS, QUERY_HEADS * HEAD_SIZE)
    query_unit = normalize(delta_query, 1.0 / math.sqrt(HEAD_SIZE))
    key_unit = normalize(delta_key, 1.0)
    inputs = (to_spans(query_unit, SPAN), to_spans(key_unit, SPAN), to_spans(delta_value.astype(jnp.float32), SPAN), gate_spans(beta_gate, SPAN), gate_spans(log_decay, SPAN))

    def span_step(carried, span_inputs):
        query_part, key_part, value_part, beta_part, log_part = span_inputs
        prepared = prepare(query_part, key_part, beta_part, log_part)
        return advance(carried, query_part, key_part, value_part, beta_part, prepared)
    start_state = jnp.zeros((DELTA_HEADS, HEAD_SIZE, HEAD_SIZE), jnp.float32)
    final_state, span_outs = lax.scan(span_step, start_state, inputs)
    delta_out = from_spans(span_outs).astype(jnp.bfloat16)
    return (attn_out, delta_out)
```

```python
import math

import jax
import jax.numpy as jnp
from jax import lax
from jax.experimental import pallas as pl
from jax.experimental.pallas import tpu as pltpu
from jax.sharding import Mesh, PartitionSpec as P

WINDOW = 1024
CHUNK = 128
HEAD = 128
EPSILON = 1e-06
MASKED = -1e30

f32 = jnp.float32
bf16 = jnp.bfloat16


def dot(left, right):
    return lax.dot_general(left, right, (((1,), (0,)), ((), ())), preferred_element_type=f32)


def dot_t(left, right):
    return lax.dot_general(left, right, (((1,), (1,)), ((), ())), preferred_element_type=f32)


def split(value):
    high = value.astype(bf16)
    return high, (value - high.astype(f32)).astype(bf16)


def wide_left(value):
    return jnp.concatenate(split(value), axis=1)


def full_product(left, right):
    size = right.shape[1]
    pair = jnp.concatenate(split(right), axis=1)
    both = dot(wide_left(left), jnp.concatenate((pair, pair), axis=0))
    return both[:, :size] + both[:, size:]


def exact_right(left, right):
    return dot(wide_left(left), jnp.concatenate((right, right), axis=0))


def invert_unit(stricts, row, col):
    size = stricts[0].shape[0]
    eye = jnp.where(row == col, 1.0, 0.0).astype(f32)
    block = 8
    same = (row // block) == (col // block)
    power = [jnp.where(same, a, 0.0) for a in stricts]
    inverse = [eye - a for a in power]
    for _ in range(2):
        power = [full_product(a, a) for a in power]
        inverse = [x + full_product(x, a) for x, a in zip(inverse, power)]
    while block < size:
        below = ((row // block) % 2 == 1) & ((col // block) == (row // block) - 1)
        joint = [full_product(jnp.where(below, a, 0.0), x) for a, x in zip(stricts, inverse)]
        inverse = [x - full_product(x, j) for x, j in zip(inverse, joint)]
        block *= 2
    return inverse


def delta_body(q_ref, k_ref, v_ref, log_ref, beta_ref, local_ref, reach_ref, state_ref):
    tokens = q_ref.shape[0]
    heads = q_ref.shape[1] // HEAD
    chunks = tokens // CHUNK
    row = lax.broadcasted_iota(jnp.int32, (CHUNK, CHUNK), 0)
    col = lax.broadcasted_iota(jnp.int32, (CHUNK, CHUNK), 1)
    parts = []
    for h in range(heads):
        for c in range(chunks):
            span = slice(c * CHUNK, (c + 1) * CHUNK)
            lanes = slice(h * HEAD, (h + 1) * HEAD)
            key = k_ref[span, lanes]
            query = q_ref[span, lanes]
            log_row = log_ref[0, h : h + 1, span]
            beta_row = beta_ref[0, h : h + 1, span]
            cum_col = jnp.sum(jnp.where(col <= row, log_row, 0.0), axis=1, keepdims=True)
            log_col = jnp.sum(jnp.where(col == row, log_row, 0.0), axis=1, keepdims=True)
            beta_col = jnp.sum(jnp.where(col == row, beta_row, 0.0), axis=1, keepdims=True)
            cum_row = jnp.sum(jnp.where(row <= col, log_col, 0.0), axis=0, keepdims=True)
            inner = dot_t(key, key)
            cross = dot_t(query, key)
            diag = jnp.where(row == col, inner, 0.0)
            key_col = lax.rsqrt(jnp.sum(diag, axis=1, keepdims=True) + EPSILON)
            key_row = lax.rsqrt(jnp.sum(diag, axis=0, keepdims=True) + EPSILON)
            wide_query = query.astype(f32)
            query_col = lax.rsqrt(
                jnp.sum(wide_query * wide_query, axis=1, keepdims=True) + EPSILON
            ) * (1.0 / math.sqrt(HEAD))
            decay = jnp.exp(jnp.where(row >= col, cum_col - cum_row, MASKED)) * key_row
            strict = jnp.where(row > col, decay * inner * (beta_col * key_col), 0.0)
            causal = decay * cross * query_col
            lead_col = jnp.exp(cum_col)
            last = cum_col[CHUNK - 1 : CHUNK, :]
            parts.append(
                dict(
                    key=key,
                    query=query,
                    strict=strict,
                    causal=causal,
                    u_row=beta_row,
                    y_row=beta_row * jnp.exp(cum_row) * key_row,
                    out_col=lead_col * query_col,
                    trail_col=jnp.exp(last - cum_col) * key_col,
                    whole=jnp.exp(last),
                    value=v_ref[span, lanes],
                )
            )
    inverses = invert_unit([p["strict"] for p in parts], row, col)
    for p, inverse in zip(parts, inverses):
        p["u"] = exact_right(inverse * p["u_row"], p["value"])
        p["y"] = exact_right(inverse * p["y_row"], p["key"])
    eye = jnp.where(row == col, 1.0, 0.0).astype(f32)
    states = [jnp.concatenate((jnp.zeros((HEAD, HEAD), f32), eye), axis=1)] * heads
    zero = jnp.zeros((CHUNK, HEAD), f32)
    for c in range(chunks):
        for h in range(heads):
            p = parts[h * chunks + c]
            span = slice(c * CHUNK, (c + 1) * CHUNK)
            lanes = slice(h * HEAD, (h + 1) * HEAD)
            state = states[h]
            high, low = split(state)
            wide = jnp.concatenate((high, low), axis=0)
            y_wide = wide_left(p["y"])
            moved = dot(y_wide, jnp.concatenate((high, high), axis=0)) + dot(
                y_wide[:, :HEAD], low
            )
            weighted = jnp.concatenate((p["u"], zero), axis=1) - moved
            seen = dot(jnp.concatenate((p["query"], p["query"]), axis=1), wide)
            near = weighted.astype(bf16)
            result = p["out_col"] * seen + dot(
                wide_left(p["causal"]), jnp.concatenate((near, near), axis=0)
            )
            local_ref[span, lanes] = result[:, :HEAD]
            reach_ref[span, lanes] = result[:, HEAD:].astype(bf16)
            key_t = p["key"].T
            kept = jnp.concatenate(split(weighted * p["trail_col"]), axis=0)
            states[h] = p["whole"] * state + dot(jnp.concatenate((key_t, key_t), axis=1), kept)
    for h in range(heads):
        state_ref[h, :HEAD, :] = states[h][:, :HEAD].T
        state_ref[h, HEAD:, :] = states[h][:, HEAD:].T


def delta_local(query, key, value, log_decay, beta_gate, heads_step=2):
    tokens, width = query.shape
    heads = width // HEAD
    steps = heads // heads_step
    lanes = heads_step * HEAD
    gates = pl.BlockSpec((1, heads_step, tokens), lambda i: (i, 0, 0))
    rows = pl.BlockSpec((tokens, lanes), lambda i: (0, i))
    return pl.pallas_call(
        delta_body,
        grid=(steps,),
        in_specs=[rows, rows, rows, gates, gates],
        out_specs=[
            rows,
            rows,
            pl.BlockSpec((heads_step, 2 * HEAD, HEAD), lambda i: (i, 0, 0)),
        ],
        out_shape=[
            jax.ShapeDtypeStruct((tokens, width), f32),
            jax.ShapeDtypeStruct((tokens, width), bf16),
            jax.ShapeDtypeStruct((heads, 2 * HEAD, HEAD), f32),
        ],
        name="delta_local",
        compiler_params=pltpu.CompilerParams(dimension_semantics=("arbitrary",)),
    )(
        query,
        key,
        value,
        log_decay.reshape(steps, heads_step, tokens),
        beta_gate.reshape(steps, heads_step, tokens),
    )


def row_product(left, right):
    high, low = split(right)
    wide = wide_left(left)
    return dot(wide, jnp.concatenate((high, high), axis=0)) + dot(wide[:, :HEAD], low)


def pack_body(pair_ref, whole_ref, out_ref):
    heads = pair_ref.shape[1]
    quarter = HEAD // 4
    row = lax.broadcasted_iota(jnp.int32, (HEAD, HEAD), 0)
    col = lax.broadcasted_iota(jnp.int32, (HEAD, HEAD), 1)
    for h in range(heads):
        joined = row_product(pair_ref[0, h], pair_ref[1, h, HEAD:, :])
        source = joined[:HEAD] + pair_ref[1, h, :HEAD, :]
        scale = whole_ref[0, h : h + 1, :].astype(bf16)
        transit = joined[HEAD:] - jnp.where(row == col, scale.astype(f32), 0.0)
        transit = transit.astype(bf16)
        source = source.astype(bf16)
        for piece in range(4):
            index = h * 4 + piece
            out_ref[index, :HEAD, :] = transit
            out_ref[index, HEAD : HEAD + quarter, :] = source[
                piece * quarter : (piece + 1) * quarter
            ]
            out_ref[index, HEAD + quarter :, :] = jnp.broadcast_to(scale, (16, HEAD))


def relay_body(message_ref, out_ref):
    quarter = HEAD // 4
    carried = jnp.zeros((quarter, HEAD), f32)
    members = message_ref.shape[0]
    for m in range(members):
        out_ref[m] = carried.astype(bf16)
        if m + 1 < members:
            transit = message_ref[m, :HEAD, :]
            source = message_ref[m, HEAD : HEAD + quarter, :].astype(f32)
            scale = message_ref[m, HEAD + quarter : HEAD + quarter + 1, :].astype(f32)
            carried = exact_right(carried, transit) + carried * scale + source


def unpack_body(start_ref, pair_ref, out_ref):
    heads = start_ref.shape[0]
    for h in range(heads):
        first = start_ref[h].astype(f32)
        out_ref[0, h] = first
        out_ref[1, h] = row_product(first, pair_ref[0, h, HEAD:, :]) + pair_ref[0, h, :HEAD, :]


def finish_body(reach_ref, local_ref, state_ref, out_ref):
    heads = state_ref.shape[0]
    for h in range(heads):
        lanes = slice(h * HEAD, (h + 1) * HEAD)
        state = state_ref[h]
        out_ref[:, lanes] = (
            local_ref[:, lanes] + dot_t(reach_ref[:, lanes], state.astype(bf16))
        ).astype(bf16)


def attend_body(first_ref, query_ref, own_ref, near_ref, far_ref, out_ref, kv_ref):
    tokens = own_ref.shape[0]
    block = query_ref.shape[0]
    group = query_ref.shape[1] // HEAD
    reach = WINDOW + block
    step = pl.program_id(1)

    @pl.when(step == 0)
    def _():
        for kv in range(2):
            kv_ref[kv, :tokens, :] = far_ref[:, kv * HEAD : (kv + 1) * HEAD]
            kv_ref[kv, tokens : 2 * tokens, :] = near_ref[:, kv * HEAD : (kv + 1) * HEAD]
            kv_ref[kv, 2 * tokens :, :] = own_ref[:, kv * HEAD : (kv + 1) * HEAD]

    begin = pl.multiple_of(step * block, block)
    keys = kv_ref[0, pl.ds(begin, reach), :]
    values = kv_ref[1, pl.ds(begin, reach), :]
    row = lax.broadcasted_iota(jnp.int32, (block, block), 0)
    col = lax.broadcasted_iota(jnp.int32, (block, block), 1)
    position = lax.broadcasted_iota(jnp.int32, (1, reach), 1) + begin
    bias = jnp.where(position >= first_ref[0], 0.0, MASKED)
    head_bias = jnp.where(col > row, 0.0, MASKED)
    tail_bias = jnp.where(col <= row, 0.0, MASKED)
    scale = 1.0 / math.sqrt(HEAD)
    for r in range(group):
        lanes = slice(r * HEAD, (r + 1) * HEAD)
        scores = dot_t(query_ref[:, lanes], keys)
        scores = jnp.concatenate(
            (
                scores[:, :block] + head_bias,
                scores[:, block:WINDOW],
                scores[:, WINDOW:] + tail_bias,
            ),
            axis=1,
        )
        scores = scores + bias
        top = jnp.max(scores, axis=1, keepdims=True)
        unnormed = jnp.exp((scores - top) * scale)
        total = jnp.sum(unnormed, axis=1, keepdims=True)
        mixed = dot(unnormed.astype(bf16), values)
        out_ref[:, lanes] = (mixed / total).astype(bf16)


def attend(first, query, own, near, far, block=128):
    tokens, width = query.shape
    groups = own.shape[1] // (2 * HEAD)
    lanes = width // groups
    kv = pl.BlockSpec((tokens, 2 * HEAD), lambda g, i, _: (0, g))
    rows = pl.BlockSpec((block, lanes), lambda g, i, _: (i, g))
    return pl.pallas_call(
        attend_body,
        grid_spec=pltpu.PrefetchScalarGridSpec(
            num_scalar_prefetch=1,
            grid=(groups, tokens // block),
            in_specs=[rows, kv, kv, kv],
            out_specs=rows,
            scratch_shapes=[pltpu.VMEM((2, WINDOW + tokens, HEAD), bf16)],
        ),
        out_shape=jax.ShapeDtypeStruct((tokens, width), bf16),
        name="attend",
        compiler_params=pltpu.CompilerParams(dimension_semantics=("arbitrary", "arbitrary")),
    )(first, query, own, near, far)


def simple_call(body, shape, name, *operands):
    return pl.pallas_call(body, out_shape=shape, name=name)(*operands)


def ring(block, axes, distance, size):
    return lax.ppermute(block, axes, [(i, (i + distance) % size) for i in range(size)])


CTX = ("y", "x", "core")
CHIPS = ("y", "x")


def local(
    attn_query, attn_key, attention_value, delta_query, delta_key, delta_value, log_decay, beta_gate
):
    tokens = attn_query.shape[0]
    size = lax.axis_size(CTX)
    index = lax.axis_index(CTX)
    kv_heads = attn_key.shape[1]
    key_value = jnp.stack((attn_key, attention_value), axis=2).reshape(tokens, -1)
    far = ring(key_value, CTX, 2, size)
    near = ring(key_value, CTX, 1, size)

    def rows(tensor):
        return tensor.reshape(tokens, -1)

    local_out, reach, state = delta_local(
        rows(delta_query), rows(delta_key), rows(delta_value), log_decay, beta_gate
    )
    heads = state.shape[0]
    half = heads // 2
    core = lax.axis_index("core")
    pair = lax.all_to_all(
        state.reshape(2, half, 2 * HEAD, HEAD), "core", split_axis=0, concat_axis=0, tiled=True
    )
    total = jnp.exp(jnp.sum(log_decay, axis=1))
    total = lax.all_to_all(
        jnp.broadcast_to(total.reshape(2, half, 1), (2, half, HEAD)),
        "core",
        split_axis=0,
        concat_axis=0,
        tiled=True,
    )
    message = simple_call(
        pack_body,
        jax.ShapeDtypeStruct((half * 4, HEAD + HEAD // 4 + 16, HEAD), bf16),
        "pack",
        pair,
        (total[0] * total[1])[None],
    )
    gathered = lax.all_to_all(message, CHIPS, split_axis=0, concat_axis=0, tiled=True)
    first = jnp.maximum(0, WINDOW - tokens * index).astype(jnp.int32).reshape(1)
    attended = attend(first, rows(attn_query), key_value, near, far)
    attn_out = lax.all_to_all(attended, "head", split_axis=0, concat_axis=1, tiled=True)
    starts = simple_call(
        relay_body,
        jax.ShapeDtypeStruct((half * 4, HEAD // 4, HEAD), bf16),
        "relay",
        gathered,
    )
    returned = lax.all_to_all(starts, CHIPS, split_axis=0, concat_axis=0, tiled=True)
    both = simple_call(
        unpack_body,
        jax.ShapeDtypeStruct((2, half, HEAD, HEAD), f32),
        "unpack",
        returned.reshape(half, HEAD, HEAD),
        pair,
    )
    incoming = lax.all_to_all(both, "core", split_axis=0, concat_axis=0, tiled=True)
    delta = simple_call(
        finish_body,
        jax.ShapeDtypeStruct(reach.shape, bf16),
        "finish",
        reach,
        local_out,
        incoming.reshape(heads, HEAD, HEAD),
    )
    delta_out = lax.all_to_all(delta, "head", split_axis=0, concat_axis=1, tiled=True)
    return (attn_out, delta_out)


def solution(mesh):
    fine = Mesh(mesh.devices.reshape(4, 4, 2, 4), ("y", "x", "core", "head"))
    cut = P(CTX, "head", None)
    gate = P("head", CTX)
    out = P((*CTX, "head"), None)
    return jax.shard_map(
        local,
        mesh=fine,
        in_specs=(cut,) * 6 + (gate, gate),
        out_specs=(out, out),
        check_vma=False,
    )
```

```python
import math

import jax
import jax.numpy as jnp
from jax import lax
from jax.experimental import pallas as pl
from jax.experimental.pallas import tpu as pltpu
from jax.sharding import Mesh, PartitionSpec as P


WINDOW = 1024
CHUNK = 128
HEAD = 128
EPSILON = 1e-06
MASKED = -1e30
STATE = 2 * HEAD + 8
ONCHIP = pl.BlockSpec(memory_space=pltpu.VMEM)
SCALAR = pl.BlockSpec(memory_space=pltpu.SMEM)

f32 = jnp.float32
bf16 = jnp.bfloat16


def dot(left, right):
    return lax.dot_general(left, right, (((1,), (0,)), ((), ())), preferred_element_type=f32)


def dot_t(left, right):
    return lax.dot_general(left, right, (((1,), (1,)), ((), ())), preferred_element_type=f32)


def split(value):
    high = value.astype(bf16)
    return high, (value - high.astype(f32)).astype(bf16)


def wide_left(value):
    return jnp.concatenate(split(value), axis=1)


def full_product(left, right):
    size = right.shape[1]
    pair = jnp.concatenate(split(right), axis=1)
    both = dot(wide_left(left), jnp.concatenate((pair, pair), axis=0))
    return both[:, :size] + both[:, size:]


def exact_right(left, right):
    return dot(wide_left(left), jnp.concatenate((right, right), axis=0))


def invert_unit(stricts, row, col):
    size = stricts[0].shape[0]
    eye = jnp.where(row == col, 1.0, 0.0).astype(f32)
    block = 8
    same = (row // block) == (col // block)
    power = [jnp.where(same, a, 0.0) for a in stricts]
    inverse = [eye - a for a in power]
    for _ in range(2):
        power = [full_product(a, a) for a in power]
        inverse = [x + full_product(x, a) for x, a in zip(inverse, power)]
    while block < size:
        below = ((row // block) % 2 == 1) & ((col // block) == (row // block) - 1)
        joint = [full_product(jnp.where(below, a, 0.0), x) for a, x in zip(stricts, inverse)]
        inverse = [x - full_product(x, j) for x, j in zip(inverse, joint)]
        block *= 2
    return inverse


def delta_body(base_ref, q_ref, k_ref, v_ref, log_ref, beta_ref, local_ref, reach_ref, state_ref):
    tokens = q_ref.shape[0]
    heads = q_ref.shape[1] // HEAD
    begin = (base_ref[0] + pl.program_id(0)) * heads
    head_index = lax.broadcasted_iota(jnp.int32, log_ref.shape, 0)
    log_rows = [
        jnp.sum(jnp.where(head_index == begin + h, log_ref[...], 0.0), axis=0, keepdims=True)
        for h in range(heads)
    ]
    beta_rows = [
        jnp.sum(jnp.where(head_index == begin + h, beta_ref[...], 0.0), axis=0, keepdims=True)
        for h in range(heads)
    ]
    chunks = tokens // CHUNK
    row = lax.broadcasted_iota(jnp.int32, (CHUNK, CHUNK), 0)
    col = lax.broadcasted_iota(jnp.int32, (CHUNK, CHUNK), 1)
    parts = []
    for h in range(heads):
        for c in range(chunks):
            span = slice(c * CHUNK, (c + 1) * CHUNK)
            lanes = slice(h * HEAD, (h + 1) * HEAD)
            key = k_ref[span, lanes]
            query = q_ref[span, lanes]
            log_row = log_rows[h][:, span]
            beta_row = beta_rows[h][:, span]
            cum_col = jnp.sum(jnp.where(col <= row, log_row, 0.0), axis=1, keepdims=True)
            log_col = jnp.sum(jnp.where(col == row, log_row, 0.0), axis=1, keepdims=True)
            beta_col = jnp.sum(jnp.where(col == row, beta_row, 0.0), axis=1, keepdims=True)
            cum_row = jnp.sum(jnp.where(row <= col, log_col, 0.0), axis=0, keepdims=True)
            inner = dot_t(key, key)
            cross = dot_t(query, key)
            diag = jnp.where(row == col, inner, 0.0)
            key_col = lax.rsqrt(jnp.sum(diag, axis=1, keepdims=True) + EPSILON)
            key_row = lax.rsqrt(jnp.sum(diag, axis=0, keepdims=True) + EPSILON)
            wide_query = query.astype(f32)
            query_col = lax.rsqrt(
                jnp.sum(wide_query * wide_query, axis=1, keepdims=True) + EPSILON
            ) * (1.0 / math.sqrt(HEAD))
            decay = jnp.exp(jnp.where(row >= col, cum_col - cum_row, MASKED)) * key_row
            strict = jnp.where(row > col, decay * inner * (beta_col * key_col), 0.0)
            causal = decay * cross * query_col
            lead_col = jnp.exp(cum_col)
            last = cum_col[CHUNK - 1 : CHUNK, :]
            parts.append(
                dict(
                    key=key,
                    query=query,
                    strict=strict,
                    causal=causal,
                    u_row=beta_row,
                    y_row=beta_row * jnp.exp(cum_row) * key_row,
                    out_col=lead_col * query_col,
                    trail_col=jnp.exp(last - cum_col) * key_col,
                    whole=jnp.exp(last),
                    value=v_ref[span, lanes],
                )
            )
    inverses = invert_unit([p["strict"] for p in parts], row, col)
    for p, inverse in zip(parts, inverses):
        p["u"] = exact_right(inverse * p["u_row"], p["value"])
        p["y"] = exact_right(inverse * p["y_row"], p["key"])
    eye = jnp.where(row == col, 1.0, 0.0).astype(f32)
    states = [jnp.concatenate((jnp.zeros((HEAD, HEAD), f32), eye), axis=1)] * heads
    zero = jnp.zeros((CHUNK, HEAD), f32)
    for c in range(chunks):
        for h in range(heads):
            p = parts[h * chunks + c]
            span = slice(c * CHUNK, (c + 1) * CHUNK)
            lanes = slice(h * HEAD, (h + 1) * HEAD)
            state = states[h]
            high, low = split(state)
            wide = jnp.concatenate((high, low), axis=0)
            y_wide = wide_left(p["y"])
            moved = dot(y_wide, jnp.concatenate((high, high), axis=0)) + dot(
                y_wide[:, :HEAD], low
            )
            weighted = jnp.concatenate((p["u"], zero), axis=1) - moved
            seen = dot(jnp.concatenate((p["query"], p["query"]), axis=1), wide)
            near, rest = split(weighted)
            causal = wide_left(p["causal"])
            result = (
                p["out_col"] * seen
                + dot(causal, jnp.concatenate((near, near), axis=0))
                + dot(causal[:, :HEAD], rest)
            )
            local_ref[span, lanes] = result[:, :HEAD]
            reach_ref[span, lanes] = result[:, HEAD:].astype(bf16)
            key_t = p["key"].T
            kept = jnp.concatenate(split(weighted * p["trail_col"]), axis=0)
            states[h] = p["whole"] * state + dot(jnp.concatenate((key_t, key_t), axis=1), kept)
    for h in range(heads):
        place = pl.program_id(0) * heads + h
        state_ref[place, :HEAD, :] = states[h][:, :HEAD].T
        state_ref[place, HEAD : 2 * HEAD, :] = states[h][:, HEAD:].T
        whole = jnp.exp(jnp.sum(log_rows[h], axis=1, keepdims=True))
        state_ref[place, 2 * HEAD :, :] = jnp.broadcast_to(whole, (8, HEAD))


def delta_local(base, query, key, value, log_decay, beta_gate, heads, heads_step=2):
    tokens = query.shape[0]
    steps = heads // heads_step
    lanes = heads_step * HEAD
    gates = pl.BlockSpec(log_decay.shape, lambda i, s: (0, 0))
    rows = pl.BlockSpec((tokens, lanes), lambda i, s: (0, s[0] + i))
    outs = pl.BlockSpec((tokens, lanes), lambda i, s: (0, i))
    return pl.pallas_call(
        delta_body,
        grid_spec=pltpu.PrefetchScalarGridSpec(
            num_scalar_prefetch=1,
            grid=(steps,),
            in_specs=[rows, rows, rows, gates, gates],
            out_specs=[
                outs,
                outs,
                ONCHIP,
            ],
        ),
        out_shape=[
            jax.ShapeDtypeStruct((tokens, heads * HEAD), f32),
            jax.ShapeDtypeStruct((tokens, heads * HEAD), bf16),
            jax.ShapeDtypeStruct((heads, STATE, HEAD), f32),
        ],
        name="delta_local",
        compiler_params=pltpu.CompilerParams(dimension_semantics=("arbitrary",)),
    )(base, query, key, value, log_decay, beta_gate)


def row_product(left, right):
    high, low = split(right)
    wide = wide_left(left)
    return dot(wide, jnp.concatenate((high, high), axis=0)) + dot(wide[:, :HEAD], low)


def pack_body(core_ref, own_ref, other_ref, out_ref, early_ref):
    heads = own_ref.shape[0]
    quarter = HEAD // 4
    row = lax.broadcasted_iota(jnp.int32, (HEAD, HEAD), 0)
    col = lax.broadcasted_iota(jnp.int32, (HEAD, HEAD), 1)
    leads = core_ref[0] == 0
    for h in range(heads):
        own = own_ref[h]
        other = other_ref[h]
        early = jnp.where(leads, own, other)
        late = jnp.where(leads, other, own)
        early_ref[h] = early
        joined = row_product(early[: 2 * HEAD], late[HEAD : 2 * HEAD])
        source = (joined[:HEAD] + late[:HEAD]).astype(bf16)
        scale = (early[2 * HEAD :] * late[2 * HEAD :])[:1].astype(bf16)
        transit = joined[HEAD:] - jnp.where(row == col, scale.astype(f32), 0.0)
        transit = transit.astype(bf16)
        for piece in range(4):
            index = h * 4 + piece
            out_ref[index, :HEAD, :] = transit
            out_ref[index, HEAD : HEAD + quarter, :] = source[
                piece * quarter : (piece + 1) * quarter
            ]
            out_ref[index, HEAD + quarter :, :] = jnp.broadcast_to(scale, (16, HEAD))


def relay_body(message_ref, out_ref):
    quarter = HEAD // 4
    carried = jnp.zeros((quarter, HEAD), f32)
    members = message_ref.shape[0]
    for m in range(members):
        out_ref[m] = carried.astype(bf16)
        if m + 1 < members:
            transit = message_ref[m, :HEAD, :]
            source = message_ref[m, HEAD : HEAD + quarter, :].astype(f32)
            scale = message_ref[m, HEAD + quarter : HEAD + quarter + 1, :].astype(f32)
            carried = exact_right(carried, transit) + carried * scale + source


def unpack_body(core_ref, start_ref, early_ref, keep_ref, send_ref):
    leads = core_ref[0] == 0
    for h in range(start_ref.shape[0]):
        start = start_ref[h]
        first = start.astype(f32)
        early = early_ref[h]
        second = row_product(first, early[HEAD : 2 * HEAD]) + early[:HEAD]
        keep_ref[h] = jnp.where(leads, first, second).astype(bf16)
        send_ref[h] = jnp.where(leads, second, first).astype(bf16)


def finish_body(reach_ref, local_ref, state_ref, out_ref):
    for h in range(state_ref.shape[0]):
        lanes = slice(h * HEAD, (h + 1) * HEAD)
        out_ref[:, lanes] = (
            local_ref[:, lanes] + dot_t(reach_ref[:, lanes], state_ref[h])
        ).astype(bf16)


def attend_body(first_ref, turn_ref, query_ref, own_ref, near_ref, far_ref, *rest):
    *out_refs, kv_ref = rest
    tokens = own_ref.shape[0]
    block = query_ref.shape[0]
    group = query_ref.shape[1] // HEAD
    reach = WINDOW + block
    step = pl.program_id(0)
    part = pl.program_id(1)

    @pl.when((step == 0) & (part == 0))
    def _():
        for kv in range(kv_ref.shape[0]):
            lanes = slice(kv * HEAD, (kv + 1) * HEAD)
            kv_ref[kv, :tokens, :] = far_ref[:, lanes]
            kv_ref[kv, tokens : 2 * tokens, :] = near_ref[:, lanes]
            kv_ref[kv, 2 * tokens :, :] = own_ref[:, lanes]

    begin = pl.multiple_of(((step + turn_ref[0]) % (tokens // block)) * block, block)
    row = lax.broadcasted_iota(jnp.int32, (block, block), 0)
    col = lax.broadcasted_iota(jnp.int32, (block, block), 1)
    scale = math.log2(math.e) / math.sqrt(HEAD)

    def run(bounded):
        keys = kv_ref[2 * part, pl.ds(begin, reach), :]
        values = kv_ref[2 * part + 1, pl.ds(begin, reach), :]
        queries = jnp.concatenate(
            [query_ref[:, r * HEAD : (r + 1) * HEAD] for r in range(group)], axis=0
        )
        everything = dot_t(queries, keys)
        position = lax.broadcasted_iota(jnp.int32, (1, reach), 1) + begin
        bias = jnp.where(position >= first_ref[0], 0.0, MASKED)
        weights = []
        totals = []
        for r in range(group):
            scores = everything[r * block : (r + 1) * block]
            if bounded:
                scores = scores + bias
            pieces = (
                jnp.where(col > row, scores[:, :block], MASKED),
                scores[:, block:WINDOW],
                jnp.where(col <= row, scores[:, WINDOW:], MASKED),
            )
            tops = [jnp.max(piece, axis=1, keepdims=True) for piece in pieces]
            top = jnp.maximum(jnp.maximum(tops[0], tops[1]), tops[2])
            powers = [jnp.exp2((piece - top) * scale) for piece in pieces]
            sums = [jnp.sum(power, axis=1, keepdims=True) for power in powers]
            totals.append(sums[0] + sums[1] + sums[2])
            weights.append(jnp.concatenate([power.astype(bf16) for power in powers], axis=1))
        mixed = dot(jnp.concatenate(weights, axis=0), values)
        result = jnp.concatenate(
            [
                (mixed[r * block : (r + 1) * block] / totals[r]).astype(bf16)
                for r in range(group)
            ],
            axis=1,
        )
        for d, out_ref in enumerate(out_refs):

            @pl.when(step == d)
            def _(out_ref=out_ref):
                for g in range(kv_ref.shape[0] // 2):

                    @pl.when(part == g)
                    def _(g=g):
                        out_ref[:, g * group * HEAD : (g + 1) * group * HEAD] = result

    @pl.when(first_ref[0] > begin)
    def _():
        run(True)

    @pl.when(first_ref[0] <= begin)
    def _():
        run(False)


def attend(first, turn, count, query, own, near, far):
    tokens, width = query.shape
    block = tokens // count
    groups = own.shape[1] // (2 * HEAD)
    lanes = width // groups
    return pl.pallas_call(
        attend_body,
        grid_spec=pltpu.PrefetchScalarGridSpec(
            num_scalar_prefetch=2,
            grid=(count, groups),
            in_specs=[
                pl.BlockSpec((block, lanes), lambda i, g, _, t: ((i + t[0]) % count, g)),
                ONCHIP,
                ONCHIP,
                ONCHIP,
            ],
            out_specs=[ONCHIP] * count,
            scratch_shapes=[pltpu.VMEM((2 * groups, WINDOW + tokens, HEAD), bf16)],
        ),
        out_shape=[jax.ShapeDtypeStruct((block, width), bf16)] * count,
        name="attend",
        compiler_params=pltpu.CompilerParams(dimension_semantics=("arbitrary", "arbitrary")),
    )(first, turn, query, own, near, far)


def join_turns_body(place_ref, *refs):
    *in_refs, out_ref, done = refs
    width = in_refs[0].shape[1]
    copies = []
    for d, in_ref in enumerate(in_refs):
        lanes = pl.ds(pl.multiple_of(place_ref[d] * width, width), width)
        copies.append(pltpu.make_async_copy(in_ref, out_ref.at[:, lanes], done.at[d]))
    for copy in copies:
        copy.start()
    for copy in copies:
        copy.wait()


def join_halves_body(place_ref, left_ref, right_ref, out_ref, done):
    count, _, width = left_ref.shape
    copies = []
    for k, in_ref in enumerate((left_ref, right_ref)):
        for d in range(count):
            lanes = pl.ds(pl.multiple_of((2 * d + place_ref[k]) * width, width), width)
            copies.append(
                pltpu.make_async_copy(in_ref.at[d], out_ref.at[:, lanes], done.at[k * count + d])
            )
    for copy in copies:
        copy.start()
    for copy in copies:
        copy.wait()


def join_call(body, copies, rows, width, place, *operands):
    return pl.pallas_call(
        body,
        in_specs=[SCALAR] + [ONCHIP] * len(operands),
        out_specs=pl.BlockSpec(memory_space=pltpu.HBM),
        out_shape=jax.ShapeDtypeStruct((rows, width), bf16),
        scratch_shapes=[pltpu.SemaphoreType.DMA((copies,))],
    )(place, *operands)


def onchip_call(body, shapes, scalars, *operands):
    return pl.pallas_call(
        body,
        in_specs=[SCALAR] * len(scalars) + [ONCHIP] * len(operands),
        out_specs=[ONCHIP] * len(shapes),
        out_shape=shapes,
    )(*scalars, *operands)


def ring(block, axes, distance, size):
    return lax.ppermute(block, axes, [(i, (i + distance) % size) for i in range(size)])


CTX = ("y", "x", "core")
CHIPS = ("y", "x")
SWAP = [(0, 1), (1, 0)]


def exchange(block, axes):
    return lax.all_to_all(block, axes, split_axis=0, concat_axis=0, tiled=True)


def local(
    attn_query, attn_key, attention_value, delta_query, delta_key, delta_value, log_decay, beta_gate
):
    tokens = attn_query.shape[0]
    size = lax.axis_size(CTX)
    index = lax.axis_index(CTX)
    core = lax.axis_index("core").astype(jnp.int32).reshape(1)
    key_value = jnp.stack((attn_key, attention_value), axis=2).reshape(tokens, -1)
    far = ring(key_value, CTX, 2, size)
    near = ring(key_value, CTX, 1, size)

    def rows(tensor):
        return tensor.reshape(tokens, -1)

    half = delta_query.shape[1] // 2
    delta_args = (rows(delta_query), rows(delta_key), rows(delta_value), log_decay, beta_gate)
    local_b, reach_b, state_b = delta_local((1 - core) * (half // 2), *delta_args, half)
    other = lax.ppermute(state_b, "core", SWAP)
    local_a, reach_a, state_a = delta_local(core * (half // 2), *delta_args, half)
    state_a, near, far = lax.optimization_barrier((state_a, near, far))
    shape = jax.ShapeDtypeStruct
    message, early = onchip_call(
        pack_body,
        [
            shape((half * 4, HEAD + HEAD // 4 + 16, HEAD), bf16),
            shape((half, STATE, HEAD), f32),
        ],
        [core],
        state_a,
        other,
    )
    gathered = exchange(message, CHIPS)
    first = jnp.maximum(0, WINDOW - tokens * index).astype(jnp.int32).reshape(1)
    count = lax.axis_size("head")
    rank = lax.axis_index("head").astype(jnp.int32).reshape(1)
    turn = tokens // count
    attended = attend(first, rank, count, rows(attn_query), key_value, near, far)
    attn = [attended[0]]
    for d in range(1, count):
        attn.append(ring(attended[d], "head", d, count))
    (starts,) = onchip_call(relay_body, [shape((half * 4, HEAD // 4, HEAD), bf16)], [], gathered)
    returned = exchange(starts, CHIPS)
    keep, send = onchip_call(
        unpack_body,
        [shape((half, HEAD, HEAD), bf16)] * 2,
        [core],
        returned.reshape(half, HEAD, HEAD),
        early,
    )
    received = lax.ppermute(send, "core", SWAP)
    halves = [shape((tokens, half * HEAD), bf16)]
    (delta_a,) = onchip_call(finish_body, halves, [], reach_a, local_a, keep)
    delta_a = exchange(delta_a.reshape(count, turn, -1), "head")
    (delta_b,) = onchip_call(finish_body, halves, [], reach_b, local_b, received)
    delta_b = exchange(delta_b.reshape(count, turn, -1), "head")
    wide = count * delta_query.shape[1] * HEAD
    places = (rank - jnp.arange(count, dtype=jnp.int32)) % count
    attn_out = join_call(join_turns_body, count, turn, wide, places, *attn)
    sides = jnp.concatenate((core, 1 - core))
    delta_out = join_call(join_halves_body, 2 * count, turn, wide, sides, delta_a, delta_b)
    return (attn_out, delta_out)


def solution(mesh):
    fine = Mesh(mesh.devices.reshape(4, 4, 2, 4), ("y", "x", "core", "head"))
    cut = P(CTX, "head", None)
    gate = P("head", CTX)
    out = P((*CTX, "head"), None)
    return jax.shard_map(
        local,
        mesh=fine,
        in_specs=(cut,) * 6 + (gate, gate),
        out_specs=(out, out),
        check_vma=False,
    )
```

```python
import math

import jax
import jax.numpy as jnp
from jax import lax
from jax.experimental import pallas as pl
from jax.experimental.pallas import tpu as pltpu
from jax.sharding import Mesh, PartitionSpec as P


WINDOW = 1024
CHUNK = 128
HEAD = 128
EPSILON = 1e-06
MASKED = -1e30
STATE = 2 * HEAD + 8
ONCHIP = pl.BlockSpec(memory_space=pltpu.VMEM)
SCALAR = pl.BlockSpec(memory_space=pltpu.SMEM)

f32 = jnp.float32
bf16 = jnp.bfloat16


def dot(left, right):
    return lax.dot_general(left, right, (((1,), (0,)), ((), ())), preferred_element_type=f32)


def dot_t(left, right):
    return lax.dot_general(left, right, (((1,), (1,)), ((), ())), preferred_element_type=f32)


def split(value):
    high = value.astype(bf16)
    return high, (value - high.astype(f32)).astype(bf16)


def wide_left(value):
    return jnp.concatenate(split(value), axis=1)


def exact_right(left, right):
    return dot(wide_left(left), jnp.concatenate((right, right), axis=0))


def invert_unit(stricts, row, col):
    size = stricts[0].shape[0]
    base = 8
    blocks = size // base
    sub = lax.broadcasted_iota(jnp.int32, (base, size), 0)
    lane = lax.broadcasted_iota(jnp.int32, (base, size), 1)
    owner = lane // base
    inside = lane % base
    inverse = []
    for a in stricts:
        small = jnp.where(owner == 0, a[:base], 0.0)
        for k in range(1, blocks):
            small = jnp.where(owner == k, a[k * base : (k + 1) * base], small)
        x = jnp.where(inside == sub, 1.0, 0.0).astype(f32)
        for r in range(base - 1):
            factor = jnp.take_along_axis(small, owner * base + r, axis=1)
            x = x - factor * x[r : r + 1, :]
        inverse.append(
            jnp.concatenate([jnp.where(owner == k, x, 0.0) for k in range(blocks)], axis=0)
        )
    near = [a.astype(bf16) for a in stricts]
    block = base
    while block < size:
        below = ((row // block) % 2 == 1) & ((col // block) == (row // block) - 1)
        mask = jnp.where(below, 1.0, 0.0).astype(bf16)
        rounded = [x.astype(bf16) for x in inverse]
        joint = [dot(a * mask, x).astype(bf16) for a, x in zip(near, rounded)]
        inverse = [x - dot(y, j) for x, y, j in zip(inverse, rounded, joint)]
        block *= 2
    eye = jnp.where(row == col, 1.0, 0.0).astype(f32)
    rounded = [x.astype(bf16) for x in inverse]
    residual = [eye - x.astype(f32) - exact_right(a, x) for a, x in zip(stricts, rounded)]
    return [x.astype(f32) + dot(x, e.astype(bf16)) for x, e in zip(rounded, residual)]


def running_sum(rows):
    lane = lax.broadcasted_iota(jnp.int32, rows.shape, 1)
    step = 1
    while step < rows.shape[1]:
        rows = rows + jnp.where(lane >= step, pltpu.roll(rows, step, 1), 0.0)
        step *= 2
    return rows


def delta_body(base_ref, q_ref, k_ref, v_ref, log_ref, beta_ref, local_ref, reach_ref, state_ref):
    tokens = q_ref.shape[0]
    heads = q_ref.shape[1] // HEAD
    chunks = tokens // CHUNK
    row = lax.broadcasted_iota(jnp.int32, (CHUNK, CHUNK), 0)
    col = lax.broadcasted_iota(jnp.int32, (CHUNK, CHUNK), 1)
    begin = (base_ref[0] + pl.program_id(0)) * heads
    pairs = [(h, c) for c in range(chunks) for h in range(heads)]
    parts = {}

    def own_heads(ref):
        picked = ref[:heads]
        for k in range(1, ref.shape[0] // heads):
            picked = jnp.where(begin == k * heads, ref[k * heads : (k + 1) * heads], picked)
        return picked

    def stack(rows):
        return jnp.concatenate(rows, axis=0)

    logs = own_heads(log_ref)
    betas = own_heads(beta_ref)
    spans = [slice(c * CHUNK, (c + 1) * CHUNK) for c in range(chunks)]
    cum = running_sum(stack([logs[:, span] for span in spans]))
    beta = stack([betas[:, span] for span in spans])
    key_rows = []
    for h, c in pairs:
        lanes = slice(h * HEAD, (h + 1) * HEAD)
        key = k_ref[spans[c], lanes]
        query = q_ref[spans[c], lanes]
        inner = dot_t(jnp.concatenate((key, query), axis=0), key)
        wide_query = query.astype(f32)
        square = jnp.sum(wide_query * wide_query, axis=1, keepdims=True)
        key_rows.append(
            jnp.sum(jnp.where(row == col, inner[:CHUNK], 0.0), axis=0, keepdims=True)
        )
        parts[h, c] = dict(
            key=key,
            query=query,
            value=v_ref[spans[c], lanes],
            inner=inner[:CHUNK],
            cross=inner[CHUNK:],
            query_col=lax.rsqrt(square + EPSILON) * (1.0 / math.sqrt(HEAD)),
        )
    key_unit = lax.rsqrt(stack(key_rows) + EPSILON)
    last = cum[:, CHUNK - 1 :]
    y_rows = beta * jnp.exp(cum) * key_unit
    cum_cols = cum.T
    lead_cols = jnp.exp(cum_cols)
    strict_cols = (beta * key_unit).T
    trail_cols = (jnp.exp(last - cum) * key_unit).T
    whole = jnp.exp(last)
    for n, pair in enumerate(pairs):
        p = parts[pair]
        at = slice(n, n + 1)
        decay = jnp.exp(jnp.where(row >= col, cum_cols[:, at] - cum[at], MASKED)) * key_unit[at]
        p["strict"] = jnp.where(row > col, decay * p["inner"] * strict_cols[:, at], 0.0)
        p["causal"] = wide_left(decay * p["cross"] * p["query_col"])
    inverses = invert_unit([parts[pair]["strict"] for pair in pairs], row, col)
    eye = row == col
    numbered = [(slice(n, n + 1), parts[pair]) for n, pair in enumerate(pairs)]
    u_wide = [wide_left(x * beta[at]) for x, (at, p) in zip(inverses, numbered)]
    y_wide = [wide_left(x * y_rows[at]) for x, (at, p) in zip(inverses, numbered)]
    twice = [jnp.concatenate((p["value"], p["value"]), axis=0) for at, p in numbered]
    u_part = [dot(x, y) for x, y in zip(u_wide, twice)]
    twice = [jnp.concatenate((p["key"], p["key"]), axis=0) for at, p in numbered]
    y_part = [dot(x, y) for x, y in zip(y_wide, twice)]
    solved = [jnp.concatenate(both, axis=1) for both in zip(u_part, y_part)]
    terms = [
        jnp.concatenate(split(x * trail_cols[:, at]), axis=0)
        for x, (at, p) in zip(solved, numbered)
    ]
    key_t = [p["key"].T for at, p in numbered]
    kept = [dot(jnp.concatenate((k, k), axis=1), x) for k, x in zip(key_t, terms)]
    halves = [split(x) for x in solved]
    near = [
        dot(p["causal"], jnp.concatenate((x[0], x[0]), axis=0))
        for x, (at, p) in zip(halves, numbered)
    ]
    rest = [dot(p["causal"][:, :HEAD], x[1]) for x, (at, p) in zip(halves, numbered)]
    near = [x + y for x, y in zip(near, rest)]
    for n, (at, p) in enumerate(numbered):
        reach = p["query"].astype(f32) * (lead_cols[:, at] * p["query_col"]) - near[n][:, HEAD:]
        p["near"] = near[n][:, :HEAD]
        p["source"] = kept[n][:, :HEAD]
        transit = jnp.where(eye, whole[at], 0.0) - kept[n][:, HEAD:]
        if pairs[n][1] == 0:
            p["reach"] = reach
            p["transit"] = transit
        else:
            p["step"] = wide_left(jnp.concatenate((transit, reach), axis=0))
    states = [None] * heads
    for h, c in pairs:
        p = parts[h, c]
        lanes = slice(h * HEAD, (h + 1) * HEAD)
        if c == 0:
            local_ref[spans[c], lanes] = p["near"]
            reach_ref[spans[c], lanes] = p["reach"].astype(bf16)
            states[h] = jnp.concatenate((p["source"], p["transit"]), axis=1)
        else:
            high, low = split(states[h])
            moved = dot(p["step"], jnp.concatenate((high, high), axis=0)) + dot(
                p["step"][:, :HEAD], low
            )
            local_ref[spans[c], lanes] = p["near"] + moved[HEAD:, :HEAD]
            reach_ref[spans[c], lanes] = moved[HEAD:, HEAD:].astype(bf16)
            states[h] = jnp.concatenate(
                (p["source"] + moved[:HEAD, :HEAD], moved[:HEAD, HEAD:]), axis=1
            )
    total = jnp.exp(jnp.sum(logs, axis=1, keepdims=True))
    for h in range(heads):
        place = pl.program_id(0) * heads + h
        state_ref[place, :HEAD, :] = states[h][:, :HEAD].T
        state_ref[place, HEAD : 2 * HEAD, :] = states[h][:, HEAD:].T
        state_ref[place, 2 * HEAD :, :] = jnp.broadcast_to(total[h : h + 1], (8, HEAD))


def delta_local(base, query, key, value, log_decay, beta_gate, heads, heads_step=4):
    tokens = query.shape[0]
    steps = heads // heads_step
    lanes = heads_step * HEAD
    gates = pl.BlockSpec(log_decay.shape, lambda i, s: (0, 0))
    rows = pl.BlockSpec((tokens, lanes), lambda i, s: (0, s[0] + i))
    outs = pl.BlockSpec((tokens, lanes), lambda i, s: (0, i))
    return pl.pallas_call(
        delta_body,
        grid_spec=pltpu.PrefetchScalarGridSpec(
            num_scalar_prefetch=1,
            grid=(steps,),
            in_specs=[rows, rows, rows, gates, gates],
            out_specs=[
                outs,
                outs,
                ONCHIP,
            ],
        ),
        out_shape=[
            jax.ShapeDtypeStruct((tokens, heads * HEAD), f32),
            jax.ShapeDtypeStruct((tokens, heads * HEAD), bf16),
            jax.ShapeDtypeStruct((heads, STATE, HEAD), f32),
        ],
        name="delta_local",
        compiler_params=pltpu.CompilerParams(dimension_semantics=("arbitrary",)),
    )(base, query, key, value, log_decay, beta_gate)


def row_product(left, right):
    high, low = split(right)
    wide = wide_left(left)
    return dot(wide, jnp.concatenate((high, high), axis=0)) + dot(wide[:, :HEAD], low)


def pack_body(core_ref, own_ref, other_ref, out_ref, early_ref):
    heads = own_ref.shape[0]
    quarter = HEAD // 4
    row = lax.broadcasted_iota(jnp.int32, (HEAD, HEAD), 0)
    col = lax.broadcasted_iota(jnp.int32, (HEAD, HEAD), 1)
    leads = core_ref[0] == 0
    for h in range(heads):
        own = own_ref[h]
        other = other_ref[h]
        early = jnp.where(leads, own, other)
        late = jnp.where(leads, other, own)
        early_ref[h] = early
        joined = row_product(early[: 2 * HEAD], late[HEAD : 2 * HEAD])
        source = (joined[:HEAD] + late[:HEAD]).astype(bf16)
        scale = (early[2 * HEAD :] * late[2 * HEAD :])[:1].astype(bf16)
        transit = joined[HEAD:] - jnp.where(row == col, scale.astype(f32), 0.0)
        transit = transit.astype(bf16)
        for piece in range(4):
            index = h * 4 + piece
            out_ref[index, :HEAD, :] = transit
            out_ref[index, HEAD : HEAD + quarter, :] = source[
                piece * quarter : (piece + 1) * quarter
            ]
            out_ref[index, HEAD + quarter :, :] = jnp.broadcast_to(scale, (16, HEAD))


def relay_body(message_ref, out_ref):
    quarter = HEAD // 4
    carried = jnp.zeros((quarter, HEAD), f32)
    members = message_ref.shape[0]
    for m in range(members):
        out_ref[m] = carried.astype(bf16)
        if m + 1 < members:
            transit = message_ref[m, :HEAD, :]
            source = message_ref[m, HEAD : HEAD + quarter, :].astype(f32)
            scale = message_ref[m, HEAD + quarter : HEAD + quarter + 1, :].astype(f32)
            carried = exact_right(carried, transit) + carried * scale + source


def unpack_body(core_ref, start_ref, early_ref, keep_ref, send_ref):
    leads = core_ref[0] == 0
    for h in range(start_ref.shape[0]):
        start = start_ref[h]
        first = start.astype(f32)
        early = early_ref[h]
        second = row_product(first, early[HEAD : 2 * HEAD]) + early[:HEAD]
        keep_ref[h] = jnp.where(leads, first, second).astype(bf16)
        send_ref[h] = jnp.where(leads, second, first).astype(bf16)


def finish_body(reach_ref, local_ref, state_ref, out_ref):
    for h in range(state_ref.shape[0]):
        lanes = slice(h * HEAD, (h + 1) * HEAD)
        out_ref[:, lanes] = (
            local_ref[:, lanes] + dot_t(reach_ref[:, lanes], state_ref[h])
        ).astype(bf16)


def attend_body(first_ref, turn_ref, query_ref, own_ref, near_ref, far_ref, *rest):
    *out_refs, kv_ref = rest
    tokens = own_ref.shape[0]
    block = query_ref.shape[0]
    group = query_ref.shape[1] // HEAD
    reach = WINDOW + block
    step = pl.program_id(0)
    part = pl.program_id(1)

    @pl.when((step == 0) & (part == 0))
    def _():
        for kv in range(kv_ref.shape[0]):
            lanes = slice(kv * HEAD, (kv + 1) * HEAD)
            kv_ref[kv, :tokens, :] = far_ref[:, lanes]
            kv_ref[kv, tokens : 2 * tokens, :] = near_ref[:, lanes]
            kv_ref[kv, 2 * tokens :, :] = own_ref[:, lanes]

    begin = pl.multiple_of(((step + turn_ref[0]) % (tokens // block)) * block, block)
    row = lax.broadcasted_iota(jnp.int32, (block, block), 0)
    col = lax.broadcasted_iota(jnp.int32, (block, block), 1)
    scale = math.log2(math.e) / math.sqrt(HEAD)

    def run(bounded):
        keys = kv_ref[2 * part, pl.ds(begin, reach), :]
        values = kv_ref[2 * part + 1, pl.ds(begin, reach), :]
        position = lax.broadcasted_iota(jnp.int32, (1, reach), 1) + begin
        bias = jnp.where(position >= first_ref[0], 0.0, MASKED)
        at_once = 2
        scored = []
        for r in range(0, group, at_once):
            queries = jnp.concatenate(
                [query_ref[:, q * HEAD : (q + 1) * HEAD] for q in range(r, r + at_once)], axis=0
            )
            scored.append(dot_t(queries, keys))
        results = []
        for everything in scored:
            weights = []
            totals = []
            for r in range(at_once):
                scores = everything[r * block : (r + 1) * block]
                if bounded:
                    scores = scores + bias
                pieces = (
                    jnp.where(col > row, scores[:, :block], MASKED),
                    scores[:, block:WINDOW],
                    jnp.where(col <= row, scores[:, WINDOW:], MASKED),
                )
                tops = [jnp.max(piece, axis=1, keepdims=True) for piece in pieces]
                top = jnp.maximum(jnp.maximum(tops[0], tops[1]), tops[2])
                powers = [jnp.exp2((piece - top) * scale) for piece in pieces]
                sums = [jnp.sum(power, axis=1, keepdims=True) for power in powers]
                totals.append(sums[0] + sums[1] + sums[2])
                weights.append(
                    jnp.concatenate([power.astype(bf16) for power in powers], axis=1)
                )
            mixed = dot(jnp.concatenate(weights, axis=0), values)
            for r in range(at_once):
                results.append((mixed[r * block : (r + 1) * block] / totals[r]).astype(bf16))
        result = jnp.concatenate(results, axis=1)
        for d, out_ref in enumerate(out_refs):

            @pl.when(step == d)
            def _(out_ref=out_ref):
                for g in range(kv_ref.shape[0] // 2):

                    @pl.when(part == g)
                    def _(g=g):
                        out_ref[:, g * group * HEAD : (g + 1) * group * HEAD] = result

    @pl.when(first_ref[0] > begin)
    def _():
        run(True)

    @pl.when(first_ref[0] <= begin)
    def _():
        run(False)


def attend(first, turn, count, query, own, near, far):
    tokens, width = query.shape
    block = tokens // count
    groups = own.shape[1] // (2 * HEAD)
    lanes = width // groups
    return pl.pallas_call(
        attend_body,
        grid_spec=pltpu.PrefetchScalarGridSpec(
            num_scalar_prefetch=2,
            grid=(count, groups),
            in_specs=[
                pl.BlockSpec((block, lanes), lambda i, g, _, t: ((i + t[0]) % count, g)),
                ONCHIP,
                ONCHIP,
                ONCHIP,
            ],
            out_specs=[ONCHIP] * count,
            scratch_shapes=[pltpu.VMEM((2 * groups, WINDOW + tokens, HEAD), bf16)],
        ),
        out_shape=[jax.ShapeDtypeStruct((block, width), bf16)] * count,
        name="attend",
        compiler_params=pltpu.CompilerParams(dimension_semantics=("arbitrary", "arbitrary")),
    )(first, turn, query, own, near, far)


def join_turns_body(place_ref, *refs):
    *in_refs, out_ref, done = refs
    width = in_refs[0].shape[1]
    copies = []
    for d, in_ref in enumerate(in_refs):
        lanes = pl.ds(pl.multiple_of(place_ref[d] * width, width), width)
        copies.append(pltpu.make_async_copy(in_ref, out_ref.at[:, lanes], done.at[d]))
    for copy in copies:
        copy.start()
    for copy in copies:
        copy.wait()


def join_halves_body(place_ref, left_ref, right_ref, out_ref, done):
    count, _, width = left_ref.shape
    copies = []
    for k, in_ref in enumerate((left_ref, right_ref)):
        for d in range(count):
            lanes = pl.ds(pl.multiple_of((2 * d + place_ref[k]) * width, width), width)
            copies.append(
                pltpu.make_async_copy(in_ref.at[d], out_ref.at[:, lanes], done.at[k * count + d])
            )
    for copy in copies:
        copy.start()
    for copy in copies:
        copy.wait()


def join_call(body, copies, rows, width, place, *operands):
    return pl.pallas_call(
        body,
        in_specs=[SCALAR] + [ONCHIP] * len(operands),
        out_specs=pl.BlockSpec(memory_space=pltpu.HBM),
        out_shape=jax.ShapeDtypeStruct((rows, width), bf16),
        scratch_shapes=[pltpu.SemaphoreType.DMA((copies,))],
    )(place, *operands)


def onchip_call(body, shapes, scalars, *operands):
    return pl.pallas_call(
        body,
        in_specs=[SCALAR] * len(scalars) + [ONCHIP] * len(operands),
        out_specs=[ONCHIP] * len(shapes),
        out_shape=shapes,
    )(*scalars, *operands)


def ring(block, axes, distance, size):
    return lax.ppermute(block, axes, [(i, (i + distance) % size) for i in range(size)])


CTX = ("y", "x", "core")
CHIPS = ("y", "x")
SWAP = [(0, 1), (1, 0)]


def exchange(block, axes):
    return lax.all_to_all(block, axes, split_axis=0, concat_axis=0, tiled=True)


def local(
    attn_query, attn_key, attention_value, delta_query, delta_key, delta_value, log_decay, beta_gate
):
    tokens = attn_query.shape[0]
    size = lax.axis_size(CTX)
    index = lax.axis_index(CTX)
    core = lax.axis_index("core").astype(jnp.int32).reshape(1)
    key_value = jnp.stack((attn_key, attention_value), axis=2).reshape(tokens, -1)
    far = ring(key_value, CTX, 2, size)
    near = ring(key_value, CTX, 1, size)

    def rows(tensor):
        return tensor.reshape(tokens, -1)

    half = delta_query.shape[1] // 2
    delta_args = (rows(delta_query), rows(delta_key), rows(delta_value), log_decay, beta_gate)
    local_b, reach_b, state_b = delta_local(1 - core, *delta_args, half)
    other = lax.ppermute(state_b, "core", SWAP)
    local_a, reach_a, state_a = delta_local(core, *delta_args, half)
    state_a, near, far = lax.optimization_barrier((state_a, near, far))
    shape = jax.ShapeDtypeStruct
    message, early = onchip_call(
        pack_body,
        [
            shape((half * 4, HEAD + HEAD // 4 + 16, HEAD), bf16),
            shape((half, STATE, HEAD), f32),
        ],
        [core],
        state_a,
        other,
    )
    gathered = exchange(message, CHIPS)
    first = jnp.maximum(0, WINDOW - tokens * index).astype(jnp.int32).reshape(1)
    count = lax.axis_size("head")
    rank = lax.axis_index("head").astype(jnp.int32).reshape(1)
    turn = tokens // count
    attended = attend(first, rank, count, rows(attn_query), key_value, near, far)
    attn = [attended[0]]
    for d in range(1, count):
        attn.append(ring(attended[d], "head", d, count))
    (starts,) = onchip_call(relay_body, [shape((half * 4, HEAD // 4, HEAD), bf16)], [], gathered)
    returned = exchange(starts, CHIPS)
    keep, send = onchip_call(
        unpack_body,
        [shape((half, HEAD, HEAD), bf16)] * 2,
        [core],
        returned.reshape(half, HEAD, HEAD),
        early,
    )
    received = lax.ppermute(send, "core", SWAP)
    halves = [shape((tokens, half * HEAD), bf16)]
    (delta_a,) = onchip_call(finish_body, halves, [], reach_a, local_a, keep)
    delta_a = exchange(delta_a.reshape(count, turn, -1), "head")
    (delta_b,) = onchip_call(finish_body, halves, [], reach_b, local_b, received)
    delta_b = exchange(delta_b.reshape(count, turn, -1), "head")
    wide = count * delta_query.shape[1] * HEAD
    places = (rank - jnp.arange(count, dtype=jnp.int32)) % count
    attn_out = join_call(join_turns_body, count, turn, wide, places, *attn)
    sides = jnp.concatenate((core, 1 - core))
    delta_out = join_call(join_halves_body, 2 * count, turn, wide, sides, delta_a, delta_b)
    return (attn_out, delta_out)


def solution(mesh):
    fine = Mesh(mesh.devices.reshape(4, 4, 2, 4), ("y", "x", "core", "head"))
    cut = P(CTX, "head", None)
    gate = P("head", CTX)
    out = P((*CTX, "head"), None)
    return jax.shard_map(
        local,
        mesh=fine,
        in_specs=(cut,) * 6 + (gate, gate),
        out_specs=(out, out),
        check_vma=False,
    )
```

```python
import math

import jax
import jax.numpy as jnp
from jax import lax
from jax.experimental import pallas as pl
from jax.experimental.pallas import tpu as pltpu
from jax.sharding import Mesh, PartitionSpec as P


WINDOW = 1024
CHUNK = 128
HEAD = 128
EPSILON = 1e-06
MASKED = -1e30
STATE = 2 * HEAD + 8
ONCHIP = pl.BlockSpec(memory_space=pltpu.VMEM)
SCALAR = pl.BlockSpec(memory_space=pltpu.SMEM)

f32 = jnp.float32
bf16 = jnp.bfloat16


def dot(left, right):
    return lax.dot_general(left, right, (((1,), (0,)), ((), ())), preferred_element_type=f32)


def dot_t(left, right):
    return lax.dot_general(left, right, (((1,), (1,)), ((), ())), preferred_element_type=f32)


def split(value):
    high = value.astype(bf16)
    return high, (value - high.astype(f32)).astype(bf16)


def wide_left(value):
    return jnp.concatenate(split(value), axis=1)


def exact_right(left, right):
    return dot(wide_left(left), jnp.concatenate((right, right), axis=0))


def invert_unit(stricts, row, col):
    size = stricts[0].shape[0]
    base = 8
    blocks = size // base
    sub = lax.broadcasted_iota(jnp.int32, (base, size), 0)
    lane = lax.broadcasted_iota(jnp.int32, (base, size), 1)
    owner = lane // base
    inside = lane % base
    inverse = []
    for a in stricts:
        small = jnp.where(owner == 0, a[:base], 0.0)
        for k in range(1, blocks):
            small = jnp.where(owner == k, a[k * base : (k + 1) * base], small)
        x = jnp.where(inside == sub, 1.0, 0.0).astype(f32)
        for r in range(base - 1):
            factor = jnp.take_along_axis(small, owner * base + r, axis=1)
            x = x - factor * x[r : r + 1, :]
        inverse.append(
            jnp.concatenate([jnp.where(owner == k, x, 0.0) for k in range(blocks)], axis=0)
        )
    near = [a.astype(bf16) for a in stricts]
    block = base
    while block < size:
        below = ((row // block) % 2 == 1) & ((col // block) == (row // block) - 1)
        mask = jnp.where(below, 1.0, 0.0).astype(bf16)
        rounded = [x.astype(bf16) for x in inverse]
        joint = [dot(a * mask, x).astype(bf16) for a, x in zip(near, rounded)]
        inverse = [x - dot(y, j) for x, y, j in zip(inverse, rounded, joint)]
        block *= 2
    eye = jnp.where(row == col, 1.0, 0.0).astype(f32)
    rounded = [x.astype(bf16) for x in inverse]
    residual = [eye - x.astype(f32) - exact_right(a, x) for a, x in zip(stricts, rounded)]
    return [x.astype(f32) + dot(x, e.astype(bf16)) for x, e in zip(rounded, residual)]


def running_sum(rows):
    lane = lax.broadcasted_iota(jnp.int32, rows.shape, 1)
    step = 1
    while step < rows.shape[1]:
        rows = rows + jnp.where(lane >= step, pltpu.roll(rows, step, 1), 0.0)
        step *= 2
    return rows


def delta_body(base_ref, q_ref, k_ref, v_ref, log_ref, beta_ref, local_ref, reach_ref, state_ref):
    tokens = q_ref.shape[0]
    heads = q_ref.shape[1] // HEAD
    chunks = tokens // CHUNK
    row = lax.broadcasted_iota(jnp.int32, (CHUNK, CHUNK), 0)
    col = lax.broadcasted_iota(jnp.int32, (CHUNK, CHUNK), 1)
    begin = (base_ref[0] + pl.program_id(0)) * heads
    pairs = [(h, c) for c in range(chunks) for h in range(heads)]
    parts = {}

    def own_heads(ref):
        picked = ref[:heads]
        for k in range(1, ref.shape[0] // heads):
            picked = jnp.where(begin == k * heads, ref[k * heads : (k + 1) * heads], picked)
        return picked

    def stack(rows):
        return jnp.concatenate(rows, axis=0)

    logs = own_heads(log_ref)
    betas = own_heads(beta_ref)
    spans = [slice(c * CHUNK, (c + 1) * CHUNK) for c in range(chunks)]
    cum = running_sum(stack([logs[:, span] for span in spans]))
    beta = stack([betas[:, span] for span in spans])
    key_rows = []
    for h, c in pairs:
        lanes = slice(h * HEAD, (h + 1) * HEAD)
        key = k_ref[spans[c], lanes]
        query = q_ref[spans[c], lanes]
        inner = dot_t(jnp.concatenate((key, query), axis=0), key)
        wide_query = query.astype(f32)
        square = jnp.sum(wide_query * wide_query, axis=1, keepdims=True)
        key_rows.append(
            jnp.sum(jnp.where(row == col, inner[:CHUNK], 0.0), axis=0, keepdims=True)
        )
        parts[h, c] = dict(
            key=key,
            query=query,
            value=v_ref[spans[c], lanes],
            inner=inner[:CHUNK],
            cross=inner[CHUNK:],
            query_col=lax.rsqrt(square + EPSILON) * (1.0 / math.sqrt(HEAD)),
        )
    key_unit = lax.rsqrt(stack(key_rows) + EPSILON)
    last = cum[:, CHUNK - 1 :]
    y_rows = beta * jnp.exp(cum) * key_unit
    cum_cols = cum.T
    lead_cols = jnp.exp(cum_cols)
    strict_cols = (beta * key_unit).T
    trail_cols = (jnp.exp(last - cum) * key_unit).T
    whole = jnp.exp(last)
    for n, pair in enumerate(pairs):
        p = parts[pair]
        at = slice(n, n + 1)
        decay = jnp.exp(jnp.where(row >= col, cum_cols[:, at] - cum[at], MASKED)) * key_unit[at]
        p["strict"] = jnp.where(row > col, decay * p["inner"] * strict_cols[:, at], 0.0)
        p["causal"] = wide_left(decay * p["cross"] * p["query_col"])
    inverses = invert_unit([parts[pair]["strict"] for pair in pairs], row, col)
    eye = row == col
    numbered = [(slice(n, n + 1), parts[pair]) for n, pair in enumerate(pairs)]
    u_wide = [wide_left(x * beta[at]) for x, (at, p) in zip(inverses, numbered)]
    y_wide = [wide_left(x * y_rows[at]) for x, (at, p) in zip(inverses, numbered)]
    twice = [jnp.concatenate((p["value"], p["value"]), axis=0) for at, p in numbered]
    u_part = [dot(x, y) for x, y in zip(u_wide, twice)]
    twice = [jnp.concatenate((p["key"], p["key"]), axis=0) for at, p in numbered]
    y_part = [dot(x, y) for x, y in zip(y_wide, twice)]
    solved = [jnp.concatenate(both, axis=1) for both in zip(u_part, y_part)]
    terms = [
        jnp.concatenate(split(x * trail_cols[:, at]), axis=0)
        for x, (at, p) in zip(solved, numbered)
    ]
    key_t = [p["key"].T for at, p in numbered]
    kept = [dot(jnp.concatenate((k, k), axis=1), x) for k, x in zip(key_t, terms)]
    halves = [split(x) for x in solved]
    near = [
        dot(p["causal"], jnp.concatenate((x[0], x[0]), axis=0))
        for x, (at, p) in zip(halves, numbered)
    ]
    rest = [dot(p["causal"][:, :HEAD], x[1]) for x, (at, p) in zip(halves, numbered)]
    near = [x + y for x, y in zip(near, rest)]
    for n, (at, p) in enumerate(numbered):
        reach = p["query"].astype(f32) * (lead_cols[:, at] * p["query_col"]) - near[n][:, HEAD:]
        p["near"] = near[n][:, :HEAD]
        p["source"] = kept[n][:, :HEAD]
        transit = jnp.where(eye, whole[at], 0.0) - kept[n][:, HEAD:]
        if pairs[n][1] == 0:
            p["reach"] = reach
            p["transit"] = transit
        else:
            p["step"] = wide_left(jnp.concatenate((transit, reach), axis=0))
    states = [None] * heads
    for h, c in pairs:
        p = parts[h, c]
        lanes = slice(h * HEAD, (h + 1) * HEAD)
        if c == 0:
            local_ref[spans[c], lanes] = p["near"]
            reach_ref[spans[c], lanes] = p["reach"].astype(bf16)
            states[h] = jnp.concatenate((p["source"], p["transit"]), axis=1)
        else:
            high, low = split(states[h])
            moved = dot(p["step"], jnp.concatenate((high, high), axis=0)) + dot(
                p["step"][:, :HEAD], low
            )
            local_ref[spans[c], lanes] = p["near"] + moved[HEAD:, :HEAD]
            reach_ref[spans[c], lanes] = moved[HEAD:, HEAD:].astype(bf16)
            states[h] = jnp.concatenate(
                (p["source"] + moved[:HEAD, :HEAD], moved[:HEAD, HEAD:]), axis=1
            )
    total = jnp.exp(jnp.sum(logs, axis=1, keepdims=True))
    for h in range(heads):
        place = pl.program_id(0) * heads + h
        state_ref[place, :HEAD, :] = states[h][:, :HEAD].T
        state_ref[place, HEAD : 2 * HEAD, :] = states[h][:, HEAD:].T
        state_ref[place, 2 * HEAD :, :] = jnp.broadcast_to(total[h : h + 1], (8, HEAD))


def delta_local(base, query, key, value, log_decay, beta_gate, heads, heads_step=4):
    tokens = query.shape[0]
    steps = heads // heads_step
    lanes = heads_step * HEAD
    gates = pl.BlockSpec(log_decay.shape, lambda i, s: (0, 0))
    rows = pl.BlockSpec((tokens, lanes), lambda i, s: (0, s[0] + i))
    outs = pl.BlockSpec((tokens, lanes), lambda i, s: (0, i))
    return pl.pallas_call(
        delta_body,
        grid_spec=pltpu.PrefetchScalarGridSpec(
            num_scalar_prefetch=1,
            grid=(steps,),
            in_specs=[rows, rows, rows, gates, gates],
            out_specs=[
                outs,
                outs,
                ONCHIP,
            ],
        ),
        out_shape=[
            jax.ShapeDtypeStruct((tokens, heads * HEAD), f32),
            jax.ShapeDtypeStruct((tokens, heads * HEAD), bf16),
            jax.ShapeDtypeStruct((heads, STATE, HEAD), f32),
        ],
        name="delta_local",
        compiler_params=pltpu.CompilerParams(dimension_semantics=("arbitrary",)),
    )(base, query, key, value, log_decay, beta_gate)


def row_product(left, right):
    high, low = split(right)
    wide = wide_left(left)
    return dot(wide, jnp.concatenate((high, high), axis=0)) + dot(wide[:, :HEAD], low)


def pack_body(core_ref, own_ref, other_ref, out_ref, early_ref):
    heads = own_ref.shape[0]
    quarter = HEAD // 4
    row = lax.broadcasted_iota(jnp.int32, (HEAD, HEAD), 0)
    col = lax.broadcasted_iota(jnp.int32, (HEAD, HEAD), 1)
    leads = core_ref[0] == 0
    for h in range(heads):
        own = own_ref[h]
        other = other_ref[h]
        early = jnp.where(leads, own, other)
        late = jnp.where(leads, other, own)
        early_ref[h] = early
        joined = row_product(early[: 2 * HEAD], late[HEAD : 2 * HEAD])
        source = (joined[:HEAD] + late[:HEAD]).astype(bf16)
        scale = (early[2 * HEAD :] * late[2 * HEAD :])[:1].astype(bf16)
        transit = joined[HEAD:] - jnp.where(row == col, scale.astype(f32), 0.0)
        transit = transit.astype(bf16)
        for piece in range(4):
            index = h * 4 + piece
            out_ref[index, :HEAD, :] = transit
            out_ref[index, HEAD : HEAD + quarter, :] = source[
                piece * quarter : (piece + 1) * quarter
            ]
            out_ref[index, HEAD + quarter :, :] = jnp.broadcast_to(scale, (16, HEAD))


def relay_body(message_ref, out_ref):
    quarter = HEAD // 4
    carried = jnp.zeros((quarter, HEAD), f32)
    members = message_ref.shape[0]
    for m in range(members):
        out_ref[m] = carried.astype(bf16)
        if m + 1 < members:
            transit = message_ref[m, :HEAD, :]
            source = message_ref[m, HEAD : HEAD + quarter, :].astype(f32)
            scale = message_ref[m, HEAD + quarter : HEAD + quarter + 1, :].astype(f32)
            carried = exact_right(carried, transit) + carried * scale + source


def unpack_body(core_ref, start_ref, early_ref, keep_ref, send_ref):
    leads = core_ref[0] == 0
    for h in range(start_ref.shape[0]):
        start = start_ref[h]
        first = start.astype(f32)
        early = early_ref[h]
        second = row_product(first, early[HEAD : 2 * HEAD]) + early[:HEAD]
        keep_ref[h] = jnp.where(leads, first, second).astype(bf16)
        send_ref[h] = jnp.where(leads, second, first).astype(bf16)


def finish_body(reach_ref, local_ref, state_ref, out_ref):
    for h in range(state_ref.shape[0]):
        lanes = slice(h * HEAD, (h + 1) * HEAD)
        out_ref[:, lanes] = (
            local_ref[:, lanes] + dot_t(reach_ref[:, lanes], state_ref[h])
        ).astype(bf16)


def attend_body(first_ref, turn_ref, query_ref, own_ref, near_ref, far_ref, *rest):
    *out_refs, kv_ref = rest
    tokens = own_ref.shape[0]
    block = query_ref.shape[0]
    group = query_ref.shape[1] // HEAD
    reach = WINDOW + block
    step = pl.program_id(0)
    part = pl.program_id(1)

    @pl.when((step == 0) & (part == 0))
    def _():
        for kv in range(kv_ref.shape[0]):
            lanes = slice(kv * HEAD, (kv + 1) * HEAD)
            kv_ref[kv, :tokens, :] = far_ref[:, lanes]
            kv_ref[kv, tokens : 2 * tokens, :] = near_ref[:, lanes]
            kv_ref[kv, 2 * tokens :, :] = own_ref[:, lanes]

    begin = pl.multiple_of(((step + turn_ref[0]) % (tokens // block)) * block, block)
    row = lax.broadcasted_iota(jnp.int32, (block, block), 0)
    col = lax.broadcasted_iota(jnp.int32, (block, block), 1)
    scale = math.log2(math.e) / math.sqrt(HEAD)

    def run(bounded):
        keys = kv_ref[2 * part, pl.ds(begin, reach), :]
        values = kv_ref[2 * part + 1, pl.ds(begin, reach), :]
        position = lax.broadcasted_iota(jnp.int32, (1, reach), 1) + begin
        bias = jnp.where(position >= first_ref[0], 0.0, MASKED)
        at_once = 2
        scored = []
        for r in range(0, group, at_once):
            queries = jnp.concatenate(
                [query_ref[:, q * HEAD : (q + 1) * HEAD] for q in range(r, r + at_once)], axis=0
            )
            scored.append(dot_t(queries, keys))
        results = []
        for everything in scored:
            weights = []
            totals = []
            for r in range(at_once):
                scores = everything[r * block : (r + 1) * block]
                if bounded:
                    scores = scores + bias
                pieces = (
                    jnp.where(col > row, scores[:, :block], MASKED),
                    scores[:, block:WINDOW],
                    jnp.where(col <= row, scores[:, WINDOW:], MASKED),
                )
                tops = [jnp.max(piece, axis=1, keepdims=True) for piece in pieces]
                top = jnp.maximum(jnp.maximum(tops[0], tops[1]), tops[2])
                powers = [jnp.exp2((piece - top) * scale) for piece in pieces]
                sums = [jnp.sum(power, axis=1, keepdims=True) for power in powers]
                totals.append(sums[0] + sums[1] + sums[2])
                weights.append(
                    jnp.concatenate([power.astype(bf16) for power in powers], axis=1)
                )
            mixed = dot(jnp.concatenate(weights, axis=0), values)
            for r in range(at_once):
                results.append((mixed[r * block : (r + 1) * block] / totals[r]).astype(bf16))
        result = jnp.concatenate(results, axis=1)
        for d, out_ref in enumerate(out_refs):

            @pl.when(step == d)
            def _(out_ref=out_ref):
                for g in range(kv_ref.shape[0] // 2):

                    @pl.when(part == g)
                    def _(g=g):
                        out_ref[:, g * group * HEAD : (g + 1) * group * HEAD] = result

    @pl.when(first_ref[0] > begin)
    def _():
        run(True)

    @pl.when(first_ref[0] <= begin)
    def _():
        run(False)


def attend(first, turn, count, query, own, near, far):
    tokens, width = query.shape
    block = tokens // count
    groups = own.shape[1] // (2 * HEAD)
    lanes = width // groups
    return pl.pallas_call(
        attend_body,
        grid_spec=pltpu.PrefetchScalarGridSpec(
            num_scalar_prefetch=2,
            grid=(count, groups),
            in_specs=[
                pl.BlockSpec((block, lanes), lambda i, g, _, t: ((i + t[0]) % count, g)),
                ONCHIP,
                ONCHIP,
                ONCHIP,
            ],
            out_specs=[ONCHIP] * count,
            scratch_shapes=[pltpu.VMEM((2 * groups, WINDOW + tokens, HEAD), bf16)],
        ),
        out_shape=[jax.ShapeDtypeStruct((block, width), bf16)] * count,
        name="attend",
        compiler_params=pltpu.CompilerParams(dimension_semantics=("arbitrary", "arbitrary")),
    )(first, turn, query, own, near, far)


def join_turns_body(rank_ref, *refs):
    *in_refs, out_ref, done = refs
    width = in_refs[0].shape[1]
    count = len(in_refs)
    copies = []
    for d, in_ref in enumerate(in_refs):
        lanes = pl.ds(pl.multiple_of((rank_ref[0] + count - d) % count * width, width), width)
        copies.append(pltpu.make_async_copy(in_ref, out_ref.at[:, lanes], done.at[d]))
    for copy in copies:
        copy.start()
    for copy in copies:
        copy.wait()


def join_halves_body(core_ref, left_ref, right_ref, out_ref, done):
    count, _, width = left_ref.shape
    copies = []
    for k, in_ref in enumerate((left_ref, right_ref)):
        for d in range(count):
            side = core_ref[0] if k == 0 else 1 - core_ref[0]
            lanes = pl.ds(pl.multiple_of((2 * d + side) * width, width), width)
            copies.append(
                pltpu.make_async_copy(in_ref.at[d], out_ref.at[:, lanes], done.at[k * count + d])
            )
    for copy in copies:
        copy.start()
    for copy in copies:
        copy.wait()


def join_call(body, copies, rows, width, place, *operands):
    return pl.pallas_call(
        body,
        in_specs=[SCALAR] + [ONCHIP] * len(operands),
        out_specs=pl.BlockSpec(memory_space=pltpu.HBM),
        out_shape=jax.ShapeDtypeStruct((rows, width), bf16),
        scratch_shapes=[pltpu.SemaphoreType.DMA((copies,))],
    )(place, *map(onchip, operands))


def onchip(operand):
    return pltpu.with_memory_space_constraint(operand, pltpu.VMEM)


def onchip_call(body, shapes, scalars, *operands):
    return pl.pallas_call(
        body,
        in_specs=[SCALAR] * len(scalars) + [ONCHIP] * len(operands),
        out_specs=[ONCHIP] * len(shapes),
        out_shape=shapes,
    )(*scalars, *map(onchip, operands))


def ring(block, axes, distance, size):
    return lax.ppermute(block, axes, [(i, (i + distance) % size) for i in range(size)])


CTX = ("y", "x", "core")
CHIPS = ("y", "x")
SWAP = [(0, 1), (1, 0)]


def exchange(block, axes):
    return lax.all_to_all(block, axes, split_axis=0, concat_axis=0, tiled=True)


def local(
    attn_query, attn_key, attention_value, delta_query, delta_key, delta_value, log_decay, beta_gate
):
    tokens = attn_query.shape[0]
    size = lax.axis_size(CTX)
    index = lax.axis_index(CTX)
    core = lax.axis_index("core").astype(jnp.int32).reshape(1)
    key_value = jnp.stack((attn_key, attention_value), axis=2).reshape(tokens, -1)
    far = ring(key_value, CTX, 2, size)
    near = ring(key_value, CTX, 1, size)

    def rows(tensor):
        return tensor.reshape(tokens, -1)

    half = delta_query.shape[1] // 2
    delta_args = (rows(delta_query), rows(delta_key), rows(delta_value), log_decay, beta_gate)
    local_b, reach_b, state_b = delta_local(1 - core, *delta_args, half)
    other = lax.ppermute(state_b, "core", SWAP)
    local_a, reach_a, state_a = delta_local(core, *delta_args, half)
    state_a, near, far = lax.optimization_barrier((state_a, near, far))
    shape = jax.ShapeDtypeStruct
    message, early = onchip_call(
        pack_body,
        [
            shape((half * 4, HEAD + HEAD // 4 + 16, HEAD), bf16),
            shape((half, STATE, HEAD), f32),
        ],
        [core],
        state_a,
        other,
    )
    gathered = exchange(message, CHIPS)
    first = jnp.maximum(0, WINDOW - tokens * index).astype(jnp.int32).reshape(1)
    count = lax.axis_size("head")
    rank = lax.axis_index("head").astype(jnp.int32).reshape(1)
    turn = tokens // count
    attended = attend(first, rank, count, rows(attn_query), key_value, near, far)
    attn = [attended[0]]
    for d in range(1, count):
        attn.append(ring(attended[d], "head", d, count))
    (starts,) = onchip_call(relay_body, [shape((half * 4, HEAD // 4, HEAD), bf16)], [], gathered)
    returned = exchange(starts, CHIPS)
    keep, send = onchip_call(
        unpack_body,
        [shape((half, HEAD, HEAD), bf16)] * 2,
        [core],
        returned.reshape(half, HEAD, HEAD),
        early,
    )
    received = lax.ppermute(send, "core", SWAP)
    halves = [shape((tokens, half * HEAD), bf16)]
    (delta_a,) = onchip_call(finish_body, halves, [], reach_a, local_a, keep)
    delta_a = exchange(delta_a.reshape(count, turn, -1), "head")
    (delta_b,) = onchip_call(finish_body, halves, [], reach_b, local_b, received)
    delta_b = exchange(delta_b.reshape(count, turn, -1), "head")
    wide = count * delta_query.shape[1] * HEAD
    attn_out = join_call(join_turns_body, count, turn, wide, rank, *attn)
    delta_out = join_call(join_halves_body, 2 * count, turn, wide, core, delta_a, delta_b)
    return (attn_out, delta_out)


def solution(mesh):
    fine = Mesh(mesh.devices.reshape(4, 4, 2, 4), ("y", "x", "core", "head"))
    cut = P(CTX, "head", None)
    gate = P("head", CTX)
    out = P((*CTX, "head"), None)
    return jax.shard_map(
        local,
        mesh=fine,
        in_specs=(cut,) * 6 + (gate, gate),
        out_specs=(out, out),
        check_vma=False,
    )
```

```python
import functools
import math

import jax
import jax.numpy as jnp
from jax import lax
from jax.experimental import pallas as pl
from jax.experimental.pallas import tpu as pltpu
from jax.sharding import Mesh, PartitionSpec as P


WINDOW = 1024
CHUNK = 128
HEAD = 128
EPSILON = 1e-06
MASKED = -1e30
STATE = 2 * HEAD + 8
ONCHIP = pl.BlockSpec(memory_space=pltpu.VMEM)
SCALAR = pl.BlockSpec(memory_space=pltpu.SMEM)

f32 = jnp.float32
bf16 = jnp.bfloat16


def dot(left, right):
    return lax.dot_general(left, right, (((1,), (0,)), ((), ())), preferred_element_type=f32)


def dot_t(left, right):
    return lax.dot_general(left, right, (((1,), (1,)), ((), ())), preferred_element_type=f32)


def split(value):
    high = value.astype(bf16)
    return high, (value - high.astype(f32)).astype(bf16)


def wide_left(value):
    return jnp.concatenate(split(value), axis=1)


def exact_right(left, right):
    return dot(wide_left(left), jnp.concatenate((right, right), axis=0))


def invert_unit(stricts, row, col):
    size = stricts[0].shape[0]
    base = 8
    blocks = size // base
    sub = lax.broadcasted_iota(jnp.int32, (base, size), 0)
    lane = lax.broadcasted_iota(jnp.int32, (base, size), 1)
    owner = lane // base
    inside = lane % base
    inverse = []
    for a in stricts:
        small = jnp.where(owner == 0, a[:base], 0.0)
        for k in range(1, blocks):
            small = jnp.where(owner == k, a[k * base : (k + 1) * base], small)
        x = jnp.where(inside == sub, 1.0, 0.0).astype(f32)
        for r in range(base - 1):
            factor = jnp.take_along_axis(small, owner * base + r, axis=1)
            x = x - factor * x[r : r + 1, :]
        inverse.append(
            jnp.concatenate([jnp.where(owner == k, x, 0.0) for k in range(blocks)], axis=0)
        )
    near = [a.astype(bf16) for a in stricts]
    block = base
    while block < size:
        below = ((row // block) % 2 == 1) & ((col // block) == (row // block) - 1)
        mask = jnp.where(below, 1.0, 0.0).astype(bf16)
        rounded = [x.astype(bf16) for x in inverse]
        joint = [dot(a * mask, x).astype(bf16) for a, x in zip(near, rounded)]
        inverse = [x - dot(y, j) for x, y, j in zip(inverse, rounded, joint)]
        block *= 2
    eye = jnp.where(row == col, 1.0, 0.0).astype(f32)
    rounded = [x.astype(bf16) for x in inverse]
    residual = [eye - x.astype(f32) - exact_right(a, x) for a, x in zip(stricts, rounded)]
    return [x.astype(f32) + dot(x, e.astype(bf16)) for x, e in zip(rounded, residual)]


def running_sum(rows):
    lane = lax.broadcasted_iota(jnp.int32, rows.shape, 1)
    step = 1
    while step < rows.shape[1]:
        rows = rows + jnp.where(lane >= step, pltpu.roll(rows, step, 1), 0.0)
        step *= 2
    return rows


def delta_body(base_ref, q_ref, k_ref, v_ref, log_ref, beta_ref, local_ref, reach_ref, state_ref):
    tokens = q_ref.shape[0]
    heads = q_ref.shape[1] // HEAD
    chunks = tokens // CHUNK
    row = lax.broadcasted_iota(jnp.int32, (CHUNK, CHUNK), 0)
    col = lax.broadcasted_iota(jnp.int32, (CHUNK, CHUNK), 1)
    begin = (base_ref[0] + pl.program_id(0)) * heads
    pairs = [(h, c) for c in range(chunks) for h in range(heads)]
    parts = {}

    def own_heads(ref):
        picked = ref[:heads]
        for k in range(1, ref.shape[0] // heads):
            picked = jnp.where(begin == k * heads, ref[k * heads : (k + 1) * heads], picked)
        return picked

    def stack(rows):
        return jnp.concatenate(rows, axis=0)

    logs = own_heads(log_ref)
    betas = own_heads(beta_ref)
    spans = [slice(c * CHUNK, (c + 1) * CHUNK) for c in range(chunks)]
    cum = running_sum(stack([logs[:, span] for span in spans]))
    beta = stack([betas[:, span] for span in spans])
    key_rows = []
    for h, c in pairs:
        lanes = slice(h * HEAD, (h + 1) * HEAD)
        key = k_ref[spans[c], lanes]
        query = q_ref[spans[c], lanes]
        inner = dot_t(jnp.concatenate((key, query), axis=0), key)
        wide_query = query.astype(f32)
        square = jnp.sum(wide_query * wide_query, axis=1, keepdims=True)
        key_rows.append(
            jnp.sum(jnp.where(row == col, inner[:CHUNK], 0.0), axis=0, keepdims=True)
        )
        parts[h, c] = dict(
            key=key,
            query=query,
            value=v_ref[spans[c], lanes],
            inner=inner[:CHUNK],
            cross=inner[CHUNK:],
            query_col=lax.rsqrt(square + EPSILON) * (1.0 / math.sqrt(HEAD)),
        )
    key_unit = lax.rsqrt(stack(key_rows) + EPSILON)
    last = cum[:, CHUNK - 1 :]
    y_rows = beta * jnp.exp(cum) * key_unit
    cum_cols = cum.T
    lead_cols = jnp.exp(cum_cols)
    strict_cols = (beta * key_unit).T
    trail_cols = (jnp.exp(last - cum) * key_unit).T
    whole = jnp.exp(last)
    for n, pair in enumerate(pairs):
        p = parts[pair]
        at = slice(n, n + 1)
        decay = jnp.exp(jnp.where(row >= col, cum_cols[:, at] - cum[at], MASKED)) * key_unit[at]
        p["strict"] = jnp.where(row > col, decay * p["inner"] * strict_cols[:, at], 0.0)
        p["causal"] = wide_left(decay * p["cross"] * p["query_col"])
    inverses = invert_unit([parts[pair]["strict"] for pair in pairs], row, col)
    eye = row == col
    numbered = [(slice(n, n + 1), parts[pair]) for n, pair in enumerate(pairs)]
    u_wide = [wide_left(x * beta[at]) for x, (at, p) in zip(inverses, numbered)]
    y_wide = [wide_left(x * y_rows[at]) for x, (at, p) in zip(inverses, numbered)]
    twice = [jnp.concatenate((p["value"], p["value"]), axis=0) for at, p in numbered]
    u_part = [dot(x, y) for x, y in zip(u_wide, twice)]
    twice = [jnp.concatenate((p["key"], p["key"]), axis=0) for at, p in numbered]
    y_part = [dot(x, y) for x, y in zip(y_wide, twice)]
    solved = [jnp.concatenate(both, axis=1) for both in zip(u_part, y_part)]
    terms = [
        jnp.concatenate(split(x * trail_cols[:, at]), axis=0)
        for x, (at, p) in zip(solved, numbered)
    ]
    key_t = [p["key"].T for at, p in numbered]
    kept = [dot(jnp.concatenate((k, k), axis=1), x) for k, x in zip(key_t, terms)]
    halves = [split(x) for x in solved]
    near = [
        dot(p["causal"], jnp.concatenate((x[0], x[0]), axis=0))
        for x, (at, p) in zip(halves, numbered)
    ]
    rest = [dot(p["causal"][:, :HEAD], x[1]) for x, (at, p) in zip(halves, numbered)]
    near = [x + y for x, y in zip(near, rest)]
    for n, (at, p) in enumerate(numbered):
        reach = p["query"].astype(f32) * (lead_cols[:, at] * p["query_col"]) - near[n][:, HEAD:]
        p["near"] = near[n][:, :HEAD]
        p["source"] = kept[n][:, :HEAD]
        transit = jnp.where(eye, whole[at], 0.0) - kept[n][:, HEAD:]
        if pairs[n][1] == 0:
            p["reach"] = reach
            p["transit"] = transit
        else:
            p["step"] = wide_left(jnp.concatenate((transit, reach), axis=0))
    states = [None] * heads
    for h, c in pairs:
        p = parts[h, c]
        lanes = slice(h * HEAD, (h + 1) * HEAD)
        if c == 0:
            local_ref[spans[c], lanes] = p["near"]
            reach_ref[spans[c], lanes] = p["reach"].astype(bf16)
            states[h] = jnp.concatenate((p["source"], p["transit"]), axis=1)
        else:
            high, low = split(states[h])
            moved = dot(p["step"], jnp.concatenate((high, high), axis=0)) + dot(
                p["step"][:, :HEAD], low
            )
            local_ref[spans[c], lanes] = p["near"] + moved[HEAD:, :HEAD]
            reach_ref[spans[c], lanes] = moved[HEAD:, HEAD:].astype(bf16)
            states[h] = jnp.concatenate(
                (p["source"] + moved[:HEAD, :HEAD], moved[:HEAD, HEAD:]), axis=1
            )
    total = jnp.exp(jnp.sum(logs, axis=1, keepdims=True))
    for h in range(heads):
        place = pl.program_id(0) * heads + h
        state_ref[place, :HEAD, :] = states[h][:, :HEAD].T
        state_ref[place, HEAD : 2 * HEAD, :] = states[h][:, HEAD:].T
        state_ref[place, 2 * HEAD :, :] = jnp.broadcast_to(total[h : h + 1], (8, HEAD))


def delta_local(base, query, key, value, log_decay, beta_gate, heads, heads_step=4):
    tokens = query.shape[0]
    steps = heads // heads_step
    lanes = heads_step * HEAD
    gates = pl.BlockSpec(log_decay.shape, lambda i, s: (0, 0))
    rows = pl.BlockSpec((tokens, lanes), lambda i, s: (0, s[0] + i))
    outs = pl.BlockSpec((tokens, lanes), lambda i, s: (0, i))
    return pl.pallas_call(
        delta_body,
        grid_spec=pltpu.PrefetchScalarGridSpec(
            num_scalar_prefetch=1,
            grid=(steps,),
            in_specs=[rows, rows, rows, gates, gates],
            out_specs=[
                outs,
                outs,
                ONCHIP,
            ],
        ),
        out_shape=[
            jax.ShapeDtypeStruct((tokens, heads * HEAD), f32),
            jax.ShapeDtypeStruct((tokens, heads * HEAD), bf16),
            jax.ShapeDtypeStruct((heads, STATE, HEAD), f32),
        ],
        name="delta_local",
        compiler_params=pltpu.CompilerParams(dimension_semantics=("arbitrary",)),
    )(base, query, key, value, log_decay, beta_gate)


def row_product(left, right):
    high, low = split(right)
    wide = wide_left(left)
    return dot(wide, jnp.concatenate((high, high), axis=0)) + dot(wide[:, :HEAD], low)


def pack_body(core_ref, own_ref, other_ref, out_ref, early_ref):
    heads = own_ref.shape[0]
    quarter = HEAD // 4
    row = lax.broadcasted_iota(jnp.int32, (HEAD, HEAD), 0)
    col = lax.broadcasted_iota(jnp.int32, (HEAD, HEAD), 1)
    leads = core_ref[0] == 0
    for h in range(heads):
        own = own_ref[h]
        other = other_ref[h]
        early = jnp.where(leads, own, other)
        late = jnp.where(leads, other, own)
        early_ref[h] = early
        joined = row_product(early[: 2 * HEAD], late[HEAD : 2 * HEAD])
        source = (joined[:HEAD] + late[:HEAD]).astype(bf16)
        scale = (early[2 * HEAD :] * late[2 * HEAD :])[:1].astype(bf16)
        transit = joined[HEAD:] - jnp.where(row == col, scale.astype(f32), 0.0)
        transit = transit.astype(bf16)
        for piece in range(4):
            index = h * 4 + piece
            out_ref[index, :HEAD, :] = transit
            out_ref[index, HEAD : HEAD + quarter, :] = source[
                piece * quarter : (piece + 1) * quarter
            ]
            out_ref[index, HEAD + quarter :, :] = jnp.broadcast_to(scale, (16, HEAD))


def relay_body(message_ref, out_ref):
    quarter = HEAD // 4
    carried = jnp.zeros((quarter, HEAD), f32)
    members = message_ref.shape[0]
    for m in range(members):
        out_ref[m] = carried.astype(bf16)
        if m + 1 < members:
            transit = message_ref[m, :HEAD, :]
            source = message_ref[m, HEAD : HEAD + quarter, :].astype(f32)
            scale = message_ref[m, HEAD + quarter : HEAD + quarter + 1, :].astype(f32)
            carried = exact_right(carried, transit) + carried * scale + source


def unpack_body(core_ref, start_ref, early_ref, keep_ref, send_ref):
    leads = core_ref[0] == 0
    for h in range(start_ref.shape[0]):
        start = start_ref[h]
        first = start.astype(f32)
        early = early_ref[h]
        second = row_product(first, early[HEAD : 2 * HEAD]) + early[:HEAD]
        keep_ref[h] = jnp.where(leads, first, second).astype(bf16)
        send_ref[h] = jnp.where(leads, second, first).astype(bf16)


def finish_body(reach_ref, local_ref, state_ref, out_ref):
    for h in range(state_ref.shape[0]):
        lanes = slice(h * HEAD, (h + 1) * HEAD)
        out_ref[:, lanes] = (
            local_ref[:, lanes] + dot_t(reach_ref[:, lanes], state_ref[h])
        ).astype(bf16)


def attend_body(turns, first_ref, rank_ref, query_ref, own_ref, near_ref, far_ref, *rest):
    *out_refs, kv_ref = rest
    tokens = own_ref.shape[0]
    block = query_ref.shape[0]
    group = query_ref.shape[1] // HEAD
    reach = WINDOW + block
    step = pl.program_id(0)
    part = pl.program_id(1)

    @pl.when((step == 0) & (part == 0))
    def _():
        for kv in range(kv_ref.shape[0]):
            lanes = slice(kv * HEAD, (kv + 1) * HEAD)
            kv_ref[kv, :tokens, :] = far_ref[:, lanes]
            kv_ref[kv, tokens : 2 * tokens, :] = near_ref[:, lanes]
            kv_ref[kv, 2 * tokens :, :] = own_ref[:, lanes]

    place = (pick(turns, step) + rank_ref[0]) % (tokens // block)
    begin = pl.multiple_of(place * block, block)
    row = lax.broadcasted_iota(jnp.int32, (block, block), 0)
    col = lax.broadcasted_iota(jnp.int32, (block, block), 1)
    scale = math.log2(math.e) / math.sqrt(HEAD)

    def run(bounded):
        keys = kv_ref[2 * part, pl.ds(begin, reach), :]
        values = kv_ref[2 * part + 1, pl.ds(begin, reach), :]
        position = lax.broadcasted_iota(jnp.int32, (1, reach), 1) + begin
        bias = jnp.where(position >= first_ref[0], 0.0, MASKED)
        at_once = 2
        scored = []
        for r in range(0, group, at_once):
            queries = jnp.concatenate(
                [query_ref[:, q * HEAD : (q + 1) * HEAD] for q in range(r, r + at_once)], axis=0
            )
            scored.append(dot_t(queries, keys))
        results = []
        for everything in scored:
            weights = []
            totals = []
            for r in range(at_once):
                scores = everything[r * block : (r + 1) * block]
                if bounded:
                    scores = scores + bias
                pieces = (
                    jnp.where(col > row, scores[:, :block], MASKED),
                    scores[:, block:WINDOW],
                    jnp.where(col <= row, scores[:, WINDOW:], MASKED),
                )
                tops = [jnp.max(piece, axis=1, keepdims=True) for piece in pieces]
                top = jnp.maximum(jnp.maximum(tops[0], tops[1]), tops[2])
                powers = [jnp.exp2((piece - top) * scale) for piece in pieces]
                sums = [jnp.sum(power, axis=1, keepdims=True) for power in powers]
                totals.append(sums[0] + sums[1] + sums[2])
                weights.append(
                    jnp.concatenate([power.astype(bf16) for power in powers], axis=1)
                )
            mixed = dot(jnp.concatenate(weights, axis=0), values)
            for r in range(at_once):
                results.append((mixed[r * block : (r + 1) * block] / totals[r]).astype(bf16))
        result = jnp.concatenate(results, axis=1)
        for d, out_ref in enumerate(out_refs):

            @pl.when(step == d)
            def _(out_ref=out_ref):
                for g in range(kv_ref.shape[0] // 2):

                    @pl.when(part == g)
                    def _(g=g):
                        out_ref[:, g * group * HEAD : (g + 1) * group * HEAD] = result

    @pl.when(first_ref[0] > begin)
    def _():
        run(True)

    @pl.when(first_ref[0] <= begin)
    def _():
        run(False)


def pick(values, step):
    chosen = values[0]
    for n, value in enumerate(values[1:], 1):
        chosen = jnp.where(step == n, value, chosen)
    return chosen


def attend(turns, first, rank, count, query, own, near, far):
    tokens, width = query.shape
    block = tokens // count
    groups = own.shape[1] // (2 * HEAD)
    lanes = width // groups
    return pl.pallas_call(
        functools.partial(attend_body, turns),
        grid_spec=pltpu.PrefetchScalarGridSpec(
            num_scalar_prefetch=2,
            grid=(len(turns), groups),
            in_specs=[
                pl.BlockSpec(
                    (block, lanes), lambda i, g, _, t: ((pick(turns, i) + t[0]) % count, g)
                ),
                ONCHIP,
                ONCHIP,
                ONCHIP,
            ],
            out_specs=[ONCHIP] * len(turns),
            scratch_shapes=[pltpu.VMEM((2 * groups, WINDOW + tokens, HEAD), bf16)],
        ),
        out_shape=[jax.ShapeDtypeStruct((block, width), bf16)] * len(turns),
        name="attend",
        compiler_params=pltpu.CompilerParams(dimension_semantics=("arbitrary", "arbitrary")),
    )(first, rank, query, own, near, far)


def join_turns_body(rank_ref, *refs):
    *in_refs, out_ref, done = refs
    width = in_refs[0].shape[1]
    count = len(in_refs)
    copies = []
    for d, in_ref in enumerate(in_refs):
        lanes = pl.ds(pl.multiple_of((rank_ref[0] + count - d) % count * width, width), width)
        copies.append(pltpu.make_async_copy(in_ref, out_ref.at[:, lanes], done.at[d]))
    for copy in copies:
        copy.start()
    for copy in copies:
        copy.wait()


def join_halves_body(core_ref, left_ref, right_ref, out_ref, done):
    count, _, width = left_ref.shape
    copies = []
    for k, in_ref in enumerate((left_ref, right_ref)):
        for d in range(count):
            side = core_ref[0] if k == 0 else 1 - core_ref[0]
            lanes = pl.ds(pl.multiple_of((2 * d + side) * width, width), width)
            copies.append(
                pltpu.make_async_copy(in_ref.at[d], out_ref.at[:, lanes], done.at[k * count + d])
            )
    for copy in copies:
        copy.start()
    for copy in copies:
        copy.wait()


def join_call(body, copies, rows, width, place, *operands):
    return pl.pallas_call(
        body,
        in_specs=[SCALAR] + [ONCHIP] * len(operands),
        out_specs=pl.BlockSpec(memory_space=pltpu.HBM),
        out_shape=jax.ShapeDtypeStruct((rows, width), bf16),
        scratch_shapes=[pltpu.SemaphoreType.DMA((copies,))],
    )(place, *map(onchip, operands))


def onchip(operand):
    return pltpu.with_memory_space_constraint(operand, pltpu.VMEM)


def onchip_call(body, shapes, scalars, *operands):
    return pl.pallas_call(
        body,
        in_specs=[SCALAR] * len(scalars) + [ONCHIP] * len(operands),
        out_specs=[ONCHIP] * len(shapes),
        out_shape=shapes,
    )(*scalars, *map(onchip, operands))


def ring(block, axes, distance, size):
    return lax.ppermute(block, axes, [(i, (i + distance) % size) for i in range(size)])


CTX = ("y", "x", "core")
CHIPS = ("y", "x")
SWAP = [(0, 1), (1, 0)]


def exchange(block, axes):
    return lax.all_to_all(block, axes, split_axis=0, concat_axis=0, tiled=True)


def local(
    attn_query, attn_key, attention_value, delta_query, delta_key, delta_value, log_decay, beta_gate
):
    tokens = attn_query.shape[0]
    size = lax.axis_size(CTX)
    index = lax.axis_index(CTX)
    core = lax.axis_index("core").astype(jnp.int32).reshape(1)
    key_value = jnp.stack((attn_key, attention_value), axis=2).reshape(tokens, -1)
    far = ring(key_value, CTX, 2, size)
    near = ring(key_value, CTX, 1, size)

    def rows(tensor):
        return tensor.reshape(tokens, -1)

    half = delta_query.shape[1] // 2
    delta_args = (rows(delta_query), rows(delta_key), rows(delta_value), log_decay, beta_gate)
    local_b, reach_b, state_b = delta_local(1 - core, *delta_args, half)
    other = lax.ppermute(state_b, "core", SWAP)
    local_a, reach_a, state_a = delta_local(core, *delta_args, half)
    state_a, near, far = lax.optimization_barrier((state_a, near, far))
    shape = jax.ShapeDtypeStruct
    message, early = onchip_call(
        pack_body,
        [
            shape((half * 4, HEAD + HEAD // 4 + 16, HEAD), bf16),
            shape((half, STATE, HEAD), f32),
        ],
        [core],
        state_a,
        other,
    )
    gathered = exchange(message, CHIPS)
    first = jnp.maximum(0, WINDOW - tokens * index).astype(jnp.int32).reshape(1)
    count = lax.axis_size("head")
    rank = lax.axis_index("head").astype(jnp.int32).reshape(1)
    turn = tokens // count
    queries = rows(attn_query)
    ahead = attend((2, 1, 3), first, rank, count, queries, key_value, near, far)
    attn = [None] * count
    for block, d in zip(ahead, (2, 1, 3)):
        attn[d] = ring(block, "head", d, count)
    (attn[0],) = attend((0,), first, rank, count, queries, key_value, near, far)
    (starts,) = onchip_call(relay_body, [shape((half * 4, HEAD // 4, HEAD), bf16)], [], gathered)
    returned = exchange(starts, CHIPS)
    keep, send = onchip_call(
        unpack_body,
        [shape((half, HEAD, HEAD), bf16)] * 2,
        [core],
        returned.reshape(half, HEAD, HEAD),
        early,
    )
    received = lax.ppermute(send, "core", SWAP)
    halves = [shape((tokens, half * HEAD), bf16)]
    (delta_a,) = onchip_call(finish_body, halves, [], reach_a, local_a, keep)
    delta_a = exchange(delta_a.reshape(count, turn, -1), "head")
    (delta_b,) = onchip_call(finish_body, halves, [], reach_b, local_b, received)
    delta_b = exchange(delta_b.reshape(count, turn, -1), "head")
    wide = count * delta_query.shape[1] * HEAD
    attn_out = join_call(join_turns_body, count, turn, wide, rank, *attn)
    delta_out = join_call(join_halves_body, 2 * count, turn, wide, core, delta_a, delta_b)
    return (attn_out, delta_out)


def solution(mesh):
    fine = Mesh(mesh.devices.reshape(4, 4, 2, 4), ("y", "x", "core", "head"))
    cut = P(CTX, "head", None)
    gate = P("head", CTX)
    out = P((*CTX, "head"), None)
    return jax.shard_map(
        local,
        mesh=fine,
        in_specs=(cut,) * 6 + (gate, gate),
        out_specs=(out, out),
        check_vma=False,
    )
```
